512 devices in a mesh: ctx: 8 (over z_hi, core), head: 64 (over z_lo, x, y).
Axes of the slice: x: 4, y: 8, z: 8 (z_hi: 4, z_lo: 2; z = z_hi * 2 + z_lo), core: 2. Of those that a mesh axis runs over, the one named last changes fastest.
Arguments:
- queries: bfloat16 [32768, 64, 128], P(('ctx', 'head')), may hold values from -6 to 6
- keys: bfloat16 [32768, 8, 128], P(('ctx', 'head')), may hold values from -6 to 6
- values: bfloat16 [32768, 8, 128], P(('ctx', 'head')), may hold values from -6 to 6
- outputs: bfloat16 [32768, 64, 128], P(('ctx', 'head')), may hold values from -6 to 6
- out_grads: bfloat16 [32768, 64, 128], P(('ctx', 'head')), may hold values from -1.5 to 1.5
- log_norms: float32 [32768, 64], P(('ctx', 'head')), may hold values from 1 to 4
- block_doc: int32 [256], replicated, may hold values from 0 to 95, never falling along the last dimension, each value on 1 to 32 neighbouring positions
Outputs:
- query_grads: bfloat16 [32768, 64, 128], P(('ctx', 'head'))
- key_grads: bfloat16 [32768, 8, 128], P(('ctx', 'head'))
- value_grads: bfloat16 [32768, 8, 128], P(('ctx', 'head'))
The draws below stay inside these ranges and needn't reach their ends.
Inputs may be any that keep to these rules, and one draw needn't show every extreme that they name: `block_doc`: block ids never fall; each document covers 1 to 32 blocks, and one covers exactly 32.
All inputs are finite; a program needn't handle non-finite values.
Results may differ from the reference program's by a relative error of at most 0.0058.
Values may be sent and summed in bfloat16 or wider, within the bound.
A program may use at most 64 MiB of HBM per device.

```python
import math
import jax
import jax.numpy as jnp
import numpy as np
from jax import lax

QUERY_HEADS = 64
KEY_VALUE_HEADS = 8
HEAD_SIZE = 128
BLK = 128
TOK_DEV = 64
WINDOW_TOKENS = 32768
NBLK = 256
MAXDOC = 32
COUNT = 96
N_HEAD = 64


def shard_levels(rng, dims, split, smallest, largest):
    loudness, own = 1.0, jax.random.fold_in(rng, 6)
    for dim, blocks in split:
        heights = jnp.exp(jax.random.uniform(jax.random.fold_in(own, dim), (blocks,), jnp.float32, smallest / len(split), largest / len(split)))
        loudness = loudness * jnp.repeat(heights, dims[dim] // blocks).reshape([-1 if axis == dim else 1 for axis in range(len(dims))])
    return loudness


def split_up(amount, total, reach, slope):
    portions = [(1 << 20) // math.isqrt(standing ** slope) + 1 for standing in range(2, amount + 1)]
    surplus, counts = total - reach - (amount - 1), [1] * (amount - 1)
    while surplus > 0:
        free = [i for i in range(amount - 1) if counts[i] < reach]
        whole, remaining = sum([portions[i] for i in free]), surplus
        for i in free:
            more = min(reach - counts[i], max(1, remaining * portions[i] // whole), surplus)
            counts[i] = counts[i] + more
            surplus = surplus - more
    return np.array([reach] + counts)


def ragged_sizes(own_key, amount, total, most, skew):
    if amount == 2:
        one = jax.random.randint(own_key, (), max(1, total - most), min(most, total - 1) + 1)
        return jnp.stack([one, total - one])
    lengths = jnp.asarray(split_up(amount, total, most, skew), jnp.int32)
    twos = (amount - 1) // 2
    donor, sink = lengths[1:1 + 2 * twos:2], lengths[2:2 + 2 * twos:2]
    margin = jnp.minimum(donor - 1, most - sink)
    passed = jax.random.randint(jax.random.fold_in(own_key, 1), (twos,), 0, 1 << 20) % (margin + 1)
    lengths = lengths.at[1:1 + 2 * twos:2].set(donor - passed).at[2:2 + 2 * twos:2].set(sink + passed)
    return lengths[jax.random.permutation(jax.random.fold_in(own_key, 2), amount)]


def scatter_about(key, dims, scale, reach, split=(), kind=jnp.bfloat16):
    factor_of = shard_levels(key, dims, split, -0.22, 0.18) if split else 1.0
    result = jax.random.normal(key, dims, jnp.float32) * scale * factor_of
    return jnp.minimum(jnp.maximum(result, -reach), reach).astype(kind)


def setup_inputs(seed: int = 0) -> dict:
    splits = jax.random.split(jax.random.key(seed), 8)
    queries = scatter_about(splits[0], (WINDOW_TOKENS, QUERY_HEADS, HEAD_SIZE), 1.0, 6.0, ((0, 512),))
    keys = scatter_about(splits[1], (WINDOW_TOKENS, KEY_VALUE_HEADS, HEAD_SIZE), 1.0, 6.0, ((0, 512),))
    values = scatter_about(splits[2], (WINDOW_TOKENS, KEY_VALUE_HEADS, HEAD_SIZE), 1.0, 6.0, ((0, 512),))
    outputs = scatter_about(splits[3], (WINDOW_TOKENS, QUERY_HEADS, HEAD_SIZE), 1.0, 6.0, ((0, 512),))
    out_grads = scatter_about(splits[4], (WINDOW_TOKENS, QUERY_HEADS, HEAD_SIZE), 0.25, 1.5, ((0, 512),))
    log_norms = jnp.clip(1.0 + 3.0 * jax.random.uniform(splits[5], (WINDOW_TOKENS, QUERY_HEADS), jnp.float32) ** shard_levels(splits[5], (WINDOW_TOKENS, QUERY_HEADS), ((0, 512),), -0.2, 0.2), 1.0, 4.0)
    block_doc = jnp.searchsorted(jnp.cumsum(ragged_sizes(splits[6], COUNT, NBLK, MAXDOC, 1)), jnp.arange(NBLK), side="right").astype(jnp.int32)
    return dict(queries=queries, keys=keys, values=values, outputs=outputs, out_grads=out_grads, log_norms=log_norms, block_doc=block_doc)


def tile_pass(q_tile, grad_tile, norm_tile, delta_tile, key_tile, value_tile, visible, scale_factor):
    scores = jnp.dot(q_tile, key_tile.T, preferred_element_type=jnp.float32) * scale_factor
    soft_probs = jnp.where(visible, jnp.exp(scores - norm_tile[:, None]), 0.0)
    grad_probs = jnp.dot(grad_tile, value_tile.T, preferred_element_type=jnp.float32)
    grad_scores = (soft_probs * (grad_probs - delta_tile[:, None])).astype(jnp.bfloat16)
    query_part = jnp.dot(grad_scores, key_tile, preferred_element_type=jnp.float32) * scale_factor
    key_part = jnp.dot(grad_scores.T, q_tile, preferred_element_type=jnp.float32) * scale_factor
    value_part = jnp.dot(soft_probs.astype(jnp.bfloat16).T, grad_tile, preferred_element_type=jnp.float32)
    return query_part, key_part, value_part


def reference(queries, keys, values, outputs, out_grads, log_norms, block_doc):
    window_length = queries.shape[0]
    group_len = TOK_DEV * N_HEAD
    tile_rows = min(512, group_len)
    span_tiles = group_len // tile_rows
    tile_count = window_length // tile_rows
    query_group_factor = QUERY_HEADS // KEY_VALUE_HEADS
    scale_factor = HEAD_SIZE ** -0.5
    deltas = jnp.sum(out_grads.astype(jnp.float32) * outputs.astype(jnp.float32), axis=-1)
    token_docs = jnp.repeat(block_doc, BLK)
    offsets = jnp.arange(tile_rows, dtype=jnp.int32)

    def per_head(head_index):
        kv_index = head_index // query_group_factor
        q_head = lax.dynamic_index_in_dim(queries, head_index, 1, keepdims=False)
        grad_head = lax.dynamic_index_in_dim(out_grads, head_index, 1, keepdims=False)
        norm_head = lax.dynamic_index_in_dim(log_norms, head_index, 1, keepdims=False)
        delta_head = lax.dynamic_index_in_dim(deltas, head_index, 1, keepdims=False)
        key_head = lax.dynamic_index_in_dim(keys, kv_index, 1, keepdims=False)
        value_head = lax.dynamic_index_in_dim(values, kv_index, 1, keepdims=False)

        def over_rows(carried, row_index):
            q_start = row_index * tile_rows
            q_tile = lax.dynamic_slice_in_dim(q_head, q_start, tile_rows, 0)
            grad_tile = lax.dynamic_slice_in_dim(grad_head, q_start, tile_rows, 0)
            norm_tile = lax.dynamic_slice_in_dim(norm_head, q_start, tile_rows, 0)
            delta_tile = lax.dynamic_slice_in_dim(delta_head, q_start, tile_rows, 0)
            docs_rows = lax.dynamic_slice_in_dim(token_docs, q_start, tile_rows, 0)

            def inner_step(offset_index, inner_state):
                col_index = row_index - span_tiles + offset_index
                in_range = col_index >= 0
                k_start = jnp.maximum(col_index, 0) * tile_rows
                docs_cols = lax.dynamic_slice_in_dim(token_docs, k_start, tile_rows, 0)
                visible = (docs_rows[:, None] == docs_cols[None, :]) & ((q_start + offsets)[:, None] >= (k_start + offsets)[None, :]) & in_range

                def update(current):
                    query_acc, key_acc, value_acc = current
                    key_tile = lax.dynamic_slice_in_dim(key_head, k_start, tile_rows, 0)
                    value_tile = lax.dynamic_slice_in_dim(value_head, k_start, tile_rows, 0)
                    query_part, key_part, value_part = tile_pass(q_tile, grad_tile, norm_tile, delta_tile, key_tile, value_tile, visible, scale_factor)
                    key_acc = lax.dynamic_update_slice_in_dim(key_acc, lax.dynamic_slice_in_dim(key_acc, k_start, tile_rows, 0) + key_part, k_start, 0)
                    value_acc = lax.dynamic_update_slice_in_dim(value_acc, lax.dynamic_slice_in_dim(value_acc, k_start, tile_rows, 0) + value_part, k_start, 0)
                    return (query_acc + query_part, key_acc, value_acc)

                return lax.cond(jnp.any(visible), update, lambda current: current, inner_state)

            key_acc, value_acc = carried
            zero_tile = jnp.zeros((tile_rows, HEAD_SIZE), jnp.float32)
            query_acc, key_acc, value_acc = lax.fori_loop(0, span_tiles + 1, inner_step, (zero_tile, key_acc, value_acc))
            return (key_acc, value_acc), query_acc.astype(jnp.bfloat16)

        zero_rows = jnp.zeros((window_length, HEAD_SIZE), jnp.float32)
        (key_acc, value_acc), query_tiles = lax.scan(over_rows, (zero_rows, zero_rows), jnp.arange(tile_count, dtype=jnp.int32))
        return query_tiles.reshape(window_length, HEAD_SIZE), key_acc.astype(jnp.bfloat16), value_acc.astype(jnp.bfloat16)

    query_heads, key_head_count, value_head_count = lax.map(per_head, jnp.arange(QUERY_HEADS, dtype=jnp.int32))
    query_grads = jnp.transpose(query_heads, (1, 0, 2))
    key_grad_total = jnp.sum(key_head_count.astype(jnp.float32).reshape(KEY_VALUE_HEADS, query_group_factor, window_length, HEAD_SIZE), axis=1)
    value_grad_total = jnp.sum(value_head_count.astype(jnp.float32).reshape(KEY_VALUE_HEADS, query_group_factor, window_length, HEAD_SIZE), axis=1)
    key_grads = jnp.transpose(key_grad_total.astype(jnp.bfloat16), (1, 0, 2))
    value_grads = jnp.transpose(value_grad_total.astype(jnp.bfloat16), (1, 0, 2))
    return (query_grads, key_grads, value_grads)
```

```python
import math
import jax
import jax.numpy as jnp
from jax import lax
from jax.experimental import pallas as pl
from jax.experimental.pallas import tpu as pltpu
from jax.sharding import PartitionSpec as P

BLK = 128
TILE = 512


def attention_kernel(
    geom_ref,
    start_ref,
    q_hbm,
    g_hbm,
    norm_ref,
    delta_ref,
    kv_hbm,
    dq_ref,
    dkv_ref,
    qbuf,
    gbuf,
    kbuf,
    vbuf,
    dkacc,
    dvacc,
    dqacc,
    sems,
):
    chunks, rows, size = q_hbm.shape
    span = kv_hbm.shape[2]
    heads = 8
    copies = [
        pltpu.make_async_copy(q_hbm, qbuf, sems.at[0]),
        pltpu.make_async_copy(g_hbm, gbuf, sems.at[1]),
    ]
    for part in range(2):
        copies.append(
            pltpu.make_async_copy(
                kv_hbm.at[part, 0], kbuf.at[pl.ds(part * span, span)], sems.at[2 + part]
            )
        )
        copies.append(
            pltpu.make_async_copy(
                kv_hbm.at[part, 1], vbuf.at[pl.ds(part * span, span)], sems.at[4 + part]
            )
        )
    for copy in copies:
        copy.start()
    pad = kbuf.shape[0] - 2 * span
    kbuf[pl.ds(2 * span, pad), :] = jnp.zeros((pad, size), kbuf.dtype)
    vbuf[pl.ds(2 * span, pad), :] = jnp.zeros((pad, size), vbuf.dtype)

    step = 512

    def clear(index, carry):
        at = pl.ds(pl.multiple_of(index * step, step), step)
        dkacc[at, :] = jnp.zeros((step, size), jnp.float32)
        dvacc[at, :] = jnp.zeros((step, size), jnp.float32)
        return carry

    lax.fori_loop(0, 2 * span // step, clear, 0)
    dkacc[pl.ds(2 * span, pad), :] = jnp.zeros((pad, size), jnp.float32)
    dvacc[pl.ds(2 * span, pad), :] = jnp.zeros((pad, size), jnp.float32)
    for copy in copies:
        copy.wait()

    scale = size**-0.5
    scale2 = scale * math.log2(math.e)
    tile_blocks = TILE // BLK
    first = geom_ref[0]
    stride = geom_ref[1]
    inner = geom_ref[2]

    def one_chunk(index, carry):
        q_rows = qbuf[index]
        g_rows = gbuf[index]
        norm = norm_ref[pl.ds(index, 1), :] * math.log2(math.e)
        delta = delta_ref[pl.ds(index, 1), :]
        block = first + stride * index
        start = start_ref[index]
        dqacc[...] = jnp.zeros_like(dqacc)

        def tile(at, visible):
            keys = kbuf[at, :]
            values = vbuf[at, :]
            nt = (((1,), (1,)), ((), ()))
            nn = (((1,), (0,)), ((), ()))
            tn = (((0,), (0,)), ((), ()))
            scores = lax.dot_general(keys, q_rows, nt, preferred_element_type=jnp.float32)
            probs = jnp.exp2(scores * scale2 - norm)
            if visible is not None:
                probs = jnp.where(visible, probs, 0.0)
            grad_probs = lax.dot_general(values, g_rows, nt, preferred_element_type=jnp.float32)
            grad_scores = (probs * (grad_probs - delta)).astype(jnp.bfloat16)
            dvacc[at, :] += lax.dot_general(
                probs.astype(jnp.bfloat16), g_rows, nn, preferred_element_type=jnp.float32
            )
            dkacc[at, :] += lax.dot_general(
                grad_scores, q_rows, nn, preferred_element_type=jnp.float32
            )
            dqacc[...] += lax.dot_general(
                keys, grad_scores, tn, preferred_element_type=jnp.float32
            )

        full = (block - start) // tile_blocks

        def full_tile(number, inner_carry):
            at = pl.ds(pl.multiple_of((start + number * tile_blocks) * BLK, BLK), TILE)
            tile(at, None)
            return inner_carry

        lax.fori_loop(0, full, full_tile, 0)
        last = (start + full * tile_blocks) * BLK
        row = lax.broadcasted_iota(jnp.int32, (TILE, rows), 0) + last
        token = lax.broadcasted_iota(jnp.int32, (TILE, rows), 1) // heads + (block * BLK + inner)
        tile(pl.ds(pl.multiple_of(last, BLK), TILE), row <= token)
        dq_ref[index] = (dqacc[...].T * scale).astype(dq_ref.dtype)
        return carry

    lax.fori_loop(0, chunks, one_chunk, 0)

    def flush(index, carry):
        for part in range(2):
            source = pl.ds(pl.multiple_of(part * span + index * step, step), step)
            target = pl.ds(pl.multiple_of(index * step, step), step)
            dkv_ref[part, 0, target, :] = (dkacc[source, :] * scale).astype(dkv_ref.dtype)
            dkv_ref[part, 1, target, :] = dvacc[source, :].astype(dkv_ref.dtype)
        return carry

    lax.fori_loop(0, span // step, flush, 0)


def attention(geom, start, q_rows, g_rows, norms, deltas, kv):
    chunks, rows, size = q_rows.shape
    span = kv.shape[2]
    long = 2 * span + TILE
    vmem = pl.BlockSpec(memory_space=pltpu.VMEM)
    smem = pl.BlockSpec(memory_space=pltpu.SMEM)
    hbm = pl.BlockSpec(memory_space=pl.ANY)
    return pl.pallas_call(
        attention_kernel,
        out_shape=(
            jax.ShapeDtypeStruct(q_rows.shape, jnp.bfloat16),
            jax.ShapeDtypeStruct(kv.shape, jnp.bfloat16),
        ),
        in_specs=[smem, smem, hbm, hbm, vmem, vmem, hbm],
        out_specs=(vmem, vmem),
        scratch_shapes=[
            pltpu.VMEM(q_rows.shape, jnp.bfloat16),
            pltpu.VMEM(q_rows.shape, jnp.bfloat16),
            pltpu.VMEM((long, size), jnp.bfloat16),
            pltpu.VMEM((long, size), jnp.bfloat16),
            pltpu.VMEM((long, size), jnp.float32),
            pltpu.VMEM((long, size), jnp.float32),
            pltpu.VMEM((size, rows), jnp.float32),
            pltpu.SemaphoreType.DMA((6,)),
        ],
        compiler_params=pltpu.CompilerParams(vmem_limit_bytes=50 * 2**20),
    )(geom, start, q_rows, g_rows, norms, deltas, kv)


def shifted(value, axis, steps):
    count = lax.axis_size(axis)
    initial, last = (max(0, -steps), min(count, count - steps))
    return lax.ppermute(value, axis, [(source, source + steps) for source in range(initial, last)])


def per_device(queries, keys, values, outputs, out_grads, log_norms, block_doc):
    tok, heads_all, size = queries.shape
    groups = keys.shape[1]
    per_group = heads_all // groups
    members = lax.axis_size("head") // groups
    across = [[g * members + y for g in range(groups)] for y in range(members)]
    along = [[g * members + y for y in range(members)] for g in range(groups)]
    chunk_rows = tok * per_group
    span = tok * groups * members
    blocks = span // BLK

    def spread(value):
        return lax.all_to_all(
            value, "head", split_axis=1, concat_axis=0, tiled=True, axis_index_groups=across
        )

    deltas = jnp.sum(out_grads.astype(jnp.float32) * outputs.astype(jnp.float32), axis=-1)
    stats = jnp.stack([log_norms, deltas]).reshape(2, tok, groups, per_group)
    stats = stats.transpose(2, 0, 1, 3).reshape(groups, 2, chunk_rows)
    stats = lax.all_to_all(
        stats, "head", split_axis=0, concat_axis=0, tiled=True, axis_index_groups=across
    )
    q_rows = spread(queries).reshape(groups, chunk_rows, size)
    g_rows = spread(out_grads).reshape(groups, chunk_rows, size)
    kv = jnp.stack([keys, values]).transpose(2, 0, 1, 3)
    kv = lax.all_to_all(
        kv, "head", split_axis=0, concat_axis=0, tiled=True, axis_index_groups=across
    )
    prior = shifted(kv, "ctx", 1)
    both = jnp.stack([prior, kv]).transpose(0, 2, 1, 3, 4)
    both = lax.all_gather(both, "head", axis_index_groups=along, axis=0)
    kv_all = both.transpose(1, 2, 3, 0, 4, 5).reshape(2, 2, span, size)

    ctx_index = lax.axis_index("ctx")
    member = lax.axis_index("head") % members
    per_chunk = members * tok // BLK
    first_block = member * tok // BLK
    base = ctx_index * blocks
    own = base + first_block + per_chunk * jnp.arange(groups, dtype=jnp.int32)
    docs = block_doc[own]
    start = jnp.sum((block_doc[None, :] < docs[:, None]).astype(jnp.int32), axis=1) - base + blocks
    geom = jnp.stack(
        [blocks + first_block, jnp.int32(per_chunk), (member * tok) % BLK]
    ).astype(jnp.int32)
    dq_rows, dkv = attention(geom, start, q_rows, g_rows, stats[:, 0], stats[:, 1], kv_all)

    query_grads = lax.all_to_all(
        dq_rows.reshape(groups * tok, per_group, size),
        "head",
        split_axis=0,
        concat_axis=1,
        tiled=True,
        axis_index_groups=across,
    )
    dkv = dkv.reshape(2, 2, groups, members, tok, size).transpose(3, 0, 1, 2, 4, 5)
    dkv = lax.all_to_all(
        dkv, "head", split_axis=0, concat_axis=0, tiled=True, axis_index_groups=along
    )
    dkv = jnp.sum(dkv.astype(jnp.float32), axis=0)
    dkv = dkv[1] + shifted(dkv[0], "ctx", -1)
    dkv = dkv.astype(jnp.bfloat16).transpose(1, 0, 2, 3)
    dkv = lax.all_to_all(
        dkv, "head", split_axis=0, concat_axis=0, tiled=True, axis_index_groups=across
    )
    dkv = dkv.transpose(1, 2, 0, 3)
    return (query_grads, dkv[0], dkv[1])


def solution(mesh):
    tokens = P(("ctx", "head"), None, None)
    return jax.shard_map(
        per_device,
        mesh=mesh,
        in_specs=(tokens, tokens, tokens, tokens, tokens, P(("ctx", "head"), None), P()),
        out_specs=(tokens, tokens, tokens),
        check_vma=False,
    )
```

```python
import math
import jax
import jax.numpy as jnp
from jax import lax
from jax.experimental import pallas as pl
from jax.experimental.pallas import tpu as pltpu
from jax.sharding import PartitionSpec as P

BLK = 128
TILE = 512


def attention_kernel(
    geom_ref,
    start_ref,
    q_hbm,
    g_hbm,
    norm_ref,
    delta_ref,
    kv_hbm,
    dq_ref,
    dkv_ref,
    qbuf,
    gbuf,
    kbuf,
    vbuf,
    dkacc,
    dvacc,
    dqacc,
    sems,
):
    chunks, rows, size = q_hbm.shape
    span = kv_hbm.shape[1] // 2
    heads = 8
    copies = [
        pltpu.make_async_copy(q_hbm, qbuf, sems.at[0]),
        pltpu.make_async_copy(g_hbm, gbuf, sems.at[1]),
    ]
    copies.append(pltpu.make_async_copy(kv_hbm.at[0], kbuf.at[pl.ds(0, 2 * span)], sems.at[2]))
    copies.append(pltpu.make_async_copy(kv_hbm.at[1], vbuf.at[pl.ds(0, 2 * span)], sems.at[3]))
    for copy in copies:
        copy.start()
    pad = kbuf.shape[0] - 2 * span
    kbuf[pl.ds(2 * span, pad), :] = jnp.zeros((pad, size), kbuf.dtype)
    vbuf[pl.ds(2 * span, pad), :] = jnp.zeros((pad, size), vbuf.dtype)

    step = 512

    def clear(index, carry):
        at = pl.ds(pl.multiple_of(index * step, step), step)
        dkacc[at, :] = jnp.zeros((step, size), jnp.float32)
        dvacc[at, :] = jnp.zeros((step, size), jnp.float32)
        return carry

    lax.fori_loop(0, 2 * span // step, clear, 0)
    dkacc[pl.ds(2 * span, pad), :] = jnp.zeros((pad, size), jnp.float32)
    dvacc[pl.ds(2 * span, pad), :] = jnp.zeros((pad, size), jnp.float32)
    for copy in copies:
        copy.wait()

    scale = size**-0.5
    scale2 = scale * math.log2(math.e)
    tile_blocks = TILE // BLK
    first = geom_ref[0]
    stride = geom_ref[1]
    inner = geom_ref[2]

    def one_chunk(index, carry):
        q_rows = qbuf[index]
        g_rows = gbuf[index]
        norm = norm_ref[pl.ds(index, 1), :] * math.log2(math.e)
        delta = delta_ref[pl.ds(index, 1), :]
        block = first + stride * index
        start = start_ref[index]
        dqacc[...] = jnp.zeros_like(dqacc)

        def tile(at, visible):
            keys = kbuf[at, :]
            values = vbuf[at, :]
            nt = (((1,), (1,)), ((), ()))
            nn = (((1,), (0,)), ((), ()))
            tn = (((0,), (0,)), ((), ()))
            scores = lax.dot_general(keys, q_rows, nt, preferred_element_type=jnp.float32)
            probs = jnp.exp2(scores * scale2 - norm)
            if visible is not None:
                probs = jnp.where(visible, probs, 0.0)
            grad_probs = lax.dot_general(values, g_rows, nt, preferred_element_type=jnp.float32)
            grad_scores = (probs * (grad_probs - delta)).astype(jnp.bfloat16)
            dvacc[at, :] += lax.dot_general(
                probs.astype(jnp.bfloat16), g_rows, nn, preferred_element_type=jnp.float32
            )
            dkacc[at, :] += lax.dot_general(
                grad_scores, q_rows, nn, preferred_element_type=jnp.float32
            )
            dqacc[...] += lax.dot_general(
                keys, grad_scores, tn, preferred_element_type=jnp.float32
            )

        full = (block - start) // tile_blocks

        def full_tile(number, inner_carry):
            at = pl.ds(pl.multiple_of((start + number * tile_blocks) * BLK, BLK), TILE)
            tile(at, None)
            return inner_carry

        lax.fori_loop(0, full, full_tile, 0)
        last = (start + full * tile_blocks) * BLK
        row = lax.broadcasted_iota(jnp.int32, (TILE, rows), 0) + last
        token = lax.broadcasted_iota(jnp.int32, (TILE, rows), 1) // heads + (block * BLK + inner)
        tile(pl.ds(pl.multiple_of(last, BLK), TILE), row <= token)
        dq_ref[index] = (dqacc[...].T * scale).astype(dq_ref.dtype)
        return carry

    lax.fori_loop(0, chunks, one_chunk, 0)

    def flush(index, carry):
        at = pl.ds(pl.multiple_of(index * step, step), step)
        dkv_ref[0, at, :] = (dkacc[at, :] * scale).astype(dkv_ref.dtype)
        dkv_ref[1, at, :] = dvacc[at, :].astype(dkv_ref.dtype)
        return carry

    lax.fori_loop(0, 2 * span // step, flush, 0)


def attention(geom, start, q_rows, g_rows, norms, deltas, kv):
    chunks, rows, size = q_rows.shape
    long = kv.shape[1] + TILE
    vmem = pl.BlockSpec(memory_space=pltpu.VMEM)
    smem = pl.BlockSpec(memory_space=pltpu.SMEM)
    hbm = pl.BlockSpec(memory_space=pl.ANY)
    return pl.pallas_call(
        attention_kernel,
        out_shape=(
            jax.ShapeDtypeStruct(q_rows.shape, jnp.bfloat16),
            jax.ShapeDtypeStruct(kv.shape, jnp.bfloat16),
        ),
        in_specs=[smem, smem, hbm, hbm, vmem, vmem, hbm],
        out_specs=(vmem, vmem),
        scratch_shapes=[
            pltpu.VMEM(q_rows.shape, jnp.bfloat16),
            pltpu.VMEM(q_rows.shape, jnp.bfloat16),
            pltpu.VMEM((long, size), jnp.bfloat16),
            pltpu.VMEM((long, size), jnp.bfloat16),
            pltpu.VMEM((long, size), jnp.float32),
            pltpu.VMEM((long, size), jnp.float32),
            pltpu.VMEM((size, rows), jnp.float32),
            pltpu.SemaphoreType.DMA((6,)),
        ],
        compiler_params=pltpu.CompilerParams(vmem_limit_bytes=50 * 2**20),
    )(geom, start, q_rows, g_rows, norms, deltas, kv)


def remote(source, target, send_sem, recv_sem, device):
    return pltpu.make_async_remote_copy(
        src_ref=source,
        dst_ref=target,
        send_sem=send_sem,
        recv_sem=recv_sem,
        device_id=device,
        device_id_type=pl.DeviceIdType.MESH,
    )


class Place:
    def __init__(self, groups, members, ranges):
        self.groups, self.members, self.ranges = groups, members, ranges
        self.ctx = lax.axis_index("ctx")
        head = lax.axis_index("head")
        self.group = head // members
        self.member = lax.rem(head, members)
        self.first_core = lax.rem(self.ctx, 2) == 0
        self.has_prior = self.ctx > 0
        self.has_next = self.ctx < ranges - 1

    def of_group(self, offset):
        return lax.rem(self.group + offset + self.groups, self.groups)

    def of_member(self, offset):
        return lax.rem(self.member + offset + self.members, self.members)

    def group_device(self, offset):
        return (self.ctx, self.of_group(offset) * self.members + self.member)

    def ring_device(self, offset):
        return (self.ctx, self.group * self.members + self.of_member(offset))

    def ctx_device(self, offset):
        return (self.ctx + offset, self.group * self.members + self.member)

    def greet(self):
        barrier = pltpu.get_barrier_semaphore()

        def hello(device):
            pl.semaphore_signal(
                barrier, inc=1, device_id=device, device_id_type=pl.DeviceIdType.MESH
            )

        for offset in range(1, self.groups):
            hello(self.group_device(offset))
        hello(self.ring_device(1))
        hello(self.ring_device(-1))

        @pl.when(self.has_prior)
        def _():
            hello(self.ctx_device(-1))

        @pl.when(self.has_next)
        def _():
            hello(self.ctx_device(1))

        extra = self.has_prior.astype(jnp.int32) + self.has_next.astype(jnp.int32)
        pl.semaphore_wait(barrier, self.groups + 1 + extra)


def depth_of(kind, direction):
    return 4 if kind == direction else 3


RING = [(kind, direction) for kind in range(2) for direction in range(2)]


def gather_kernel(
    ranges,
    q_in,
    g_in,
    kv_in,
    stat_in,
    q_out,
    g_out,
    kv_out,
    stat_out,
    near_send,
    near_recv,
    home,
    ring_send,
    ring_recv,
    ctx_send,
    ctx_recv,
):
    groups, members = kv_out.shape[2], kv_out.shape[3]
    here = Place(groups, members, ranges)
    group, member = here.group, here.member
    per_group = q_out.shape[2]

    def pieces(owner, origin):
        heads = pl.ds(pl.multiple_of(owner * per_group, per_group), per_group)
        return [
            (kv_in.at[owner], kv_out.at[:, 1, origin, member]),
            (stat_in.at[owner], stat_out.at[origin]),
            (g_in.at[:, heads, :], g_out.at[origin]),
            (q_in.at[:, heads, :], q_out.at[origin]),
        ]

    local = [
        pltpu.make_async_copy(source, target, home.at[index])
        for index, (source, target) in enumerate(pieces(group, group))
    ]
    for copy in local:
        copy.start()
    here.greet()

    def near(index, offset):
        source, target = pieces(here.of_group(offset), group)[index]
        return remote(
            source,
            target,
            near_send.at[index, offset - 1],
            near_recv.at[index, offset - 1],
            here.group_device(offset),
        )

    def near_arrival(index, offset):
        target = pieces(group, here.of_group(-offset))[index][1]
        return remote(
            target,
            target,
            near_send.at[index, offset - 1],
            near_recv.at[index, offset - 1],
            here.group_device(-offset),
        )

    for index in range(4):
        for offset in range(1, groups):
            near(index, offset).start()

    def piece(part, kind, offset):
        return kv_out.at[kind, part, :, here.of_member(offset)]

    def hop(part, kind, direction, step):
        sign = 1 - 2 * direction
        block = piece(part, kind, -sign * (step - 1))
        at = (part, kind, direction, step - 1)
        return remote(block, block, ring_send.at[at], ring_recv.at[at], here.ring_device(sign))

    def arrival(part, kind, direction, step):
        sign = 1 - 2 * direction
        block = piece(part, kind, -sign * step)
        at = (part, kind, direction, step - 1)
        return remote(block, block, ring_send.at[at], ring_recv.at[at], here.ring_device(-sign))

    def onward(kind, offset):
        at = (kind, offset % members)
        return remote(
            piece(1, kind, offset),
            piece(0, kind, offset),
            ctx_send.at[at],
            ctx_recv.at[at],
            here.ctx_device(1),
        )

    def from_prior(kind, offset):
        at = (kind, offset % members)
        block = piece(0, kind, offset)
        return remote(block, block, ctx_send.at[at], ctx_recv.at[at], here.ctx_device(-1))

    local[0].wait()
    for offset in range(1, groups):
        near_arrival(0, offset).wait_recv()
    for kind, direction in RING:
        hop(1, kind, direction, 1).start()

    @pl.when(here.has_next)
    def _():
        for kind in range(2):
            onward(kind, 0).start()

    rings_prior = jnp.logical_and(here.first_core, here.has_prior)
    takes_prior = jnp.logical_not(here.first_core)

    def advance(part, step):
        for kind, direction in RING:
            depth = depth_of(kind, direction)
            if step <= depth:
                arrival(part, kind, direction, step).wait_recv()
                if step < depth:
                    hop(part, kind, direction, step + 1).start()
                if part == 1:

                    @pl.when(here.first_core)
                    def _():
                        onward(kind, (2 * direction - 1) * step).start()

    advance(1, 1)

    @pl.when(rings_prior)
    def _():
        for kind in range(2):
            from_prior(kind, 0).wait_recv()
        for kind, direction in RING:
            hop(0, kind, direction, 1).start()

    for step in range(1, 5):
        if step < 4:
            advance(1, step + 1)

        @pl.when(rings_prior)
        def _():
            advance(0, step)

    @pl.when(takes_prior)
    def _():
        for kind in range(2):
            for offset in range(members):
                from_prior(kind, offset).wait_recv()

    for copy in local[1:]:
        copy.wait()
    for index in range(1, 4):
        for offset in range(1, groups):
            near_arrival(index, offset).wait_recv()

    for index in range(4):
        for offset in range(1, groups):
            near(index, offset).wait_send()
    for kind, direction in RING:
        for step in range(1, depth_of(kind, direction) + 1):
            hop(1, kind, direction, step).wait_send()

    @pl.when(rings_prior)
    def _():
        for kind, direction in RING:
            for step in range(1, depth_of(kind, direction) + 1):
                hop(0, kind, direction, step).wait_send()

    @pl.when(here.has_next)
    def _():
        for kind in range(2):
            onward(kind, 0).wait_send()

    @pl.when(here.first_core)
    def _():
        for kind in range(2):
            for offset in range(1, members):
                onward(kind, offset).wait_send()


def gather(queries, out_grads, kv, stats, members):
    tok, heads_all, size = queries.shape
    groups = kv.shape[0]
    per_group = heads_all // groups
    hbm = pl.BlockSpec(memory_space=pl.ANY)
    rows = jax.ShapeDtypeStruct((groups, tok, per_group, size), queries.dtype)
    return pl.pallas_call(
        lambda *refs: gather_kernel(lax.axis_size("ctx"), *refs),
        out_shape=(
            rows,
            rows,
            jax.ShapeDtypeStruct((2, 2, groups, members, tok, size), kv.dtype),
            jax.ShapeDtypeStruct(stats.shape, stats.dtype),
        ),
        in_specs=[hbm] * 4,
        out_specs=(hbm,) * 4,
        scratch_shapes=[
            pltpu.SemaphoreType.DMA((4, groups - 1)),
            pltpu.SemaphoreType.DMA((4, groups - 1)),
            pltpu.SemaphoreType.DMA((4,)),
            pltpu.SemaphoreType.DMA((2, 2, 2, 4)),
            pltpu.SemaphoreType.DMA((2, 2, 2, 4)),
            pltpu.SemaphoreType.DMA((2, members)),
            pltpu.SemaphoreType.DMA((2, members)),
        ],
        compiler_params=pltpu.CompilerParams(
            collective_id=0, has_side_effects=True, vmem_limit_bytes=8 * 2**20
        ),
    )(queries, out_grads, kv, stats)


def reduce_kernel(
    ranges,
    dq_in,
    dkv_in,
    dq_out,
    dkv_out,
    part,
    extra,
    got,
    sent,
    handed,
    owed,
    total,
    near_send,
    near_recv,
    home,
    ring_send,
    ring_recv,
    ctx_send,
    ctx_recv,
    back_send,
    back_recv,
):
    groups, members = dkv_in.shape[2], dkv_in.shape[3]
    here = Place(groups, members, ranges)
    group, member = here.group, here.member
    per_group = dq_in.shape[2]
    f32 = jnp.float32

    load = pltpu.make_async_copy(dkv_in, part, home.at[0])
    load.start()

    def dq_pair(owner, origin):
        heads = pl.ds(pl.multiple_of(origin * per_group, per_group), per_group)
        return dq_in.at[owner], dq_out.at[:, heads, :]

    def dkv_pair(owner, origin):
        return total.at[:, owner], dkv_out.at[:, origin]

    dq_local = pltpu.make_async_copy(*dq_pair(group, group), home.at[1])
    dq_local.start()
    here.greet()

    rings_prior = jnp.logical_and(here.first_core, here.has_prior)
    second_core = jnp.logical_not(here.first_core)
    takes_back = jnp.logical_and(second_core, here.has_next)

    def sibling(kind):
        return remote(
            dkv_in.at[kind, 0],
            extra.at[kind],
            ctx_send.at[kind],
            ctx_recv.at[kind],
            here.ctx_device(-1),
        )

    def from_sibling(kind):
        return remote(
            extra.at[kind], extra.at[kind], ctx_send.at[kind], ctx_recv.at[kind], here.ctx_device(1)
        )

    @pl.when(second_core)
    def _():
        for kind in range(2):
            sibling(kind).start()

    def near(index, offset):
        pair = (dq_pair, dkv_pair)[index]
        source, target = pair(here.of_group(offset), group)
        at = (index, offset - 1)
        return remote(source, target, near_send.at[at], near_recv.at[at], here.group_device(offset))

    def near_arrival(index, offset):
        pair = (dq_pair, dkv_pair)[index]
        target = pair(group, here.of_group(-offset))[1]
        at = (index, offset - 1)
        return remote(target, target, near_send.at[at], near_recv.at[at], here.group_device(-offset))

    for offset in range(1, groups):
        near(0, offset).start()

    def hop(which, kind, direction, step):
        sign = 1 - 2 * direction
        at = (which, kind, direction, step - 1)
        return remote(
            sent.at[at], got.at[at], ring_send.at[at], ring_recv.at[at], here.ring_device(sign)
        )

    def arrival(which, kind, direction, step):
        sign = 1 - 2 * direction
        at = (which, kind, direction, step - 1)
        return remote(
            got.at[at], got.at[at], ring_send.at[at], ring_recv.at[at], here.ring_device(-sign)
        )

    def mine(which, kind, j, owner):
        value = part[kind, which, j, owner].astype(f32)
        if which == 1:
            value = value + extra[kind, j, owner].astype(f32)
        return value

    def forward(which, step):
        for kind, direction in RING:
            depth = depth_of(kind, direction)
            if step > depth:
                continue
            sign = 1 - 2 * direction
            owner = here.of_member(sign * (depth - step + 1))
            if step > 1:
                arrival(which, kind, direction, step - 1).wait_recv()

            def add(j, carry):
                value = mine(which, kind, j, owner)
                if step > 1:
                    value = value + got[which, kind, direction, step - 2, j].astype(f32)
                sent[which, kind, direction, step - 1, j] = value.astype(sent.dtype)
                return carry

            lax.fori_loop(0, groups, add, 0)
            hop(which, kind, direction, step).start()

    def last(which, kind, j):
        value = mine(which, kind, j, member)
        for direction in range(2):
            depth = depth_of(kind, direction)
            value = value + got[which, kind, direction, depth - 1, j].astype(f32)
        return value

    def back(kind):
        return remote(
            handed.at[kind],
            owed.at[kind],
            back_send.at[kind],
            back_recv.at[kind],
            here.ctx_device(-1),
        )

    def from_back(kind):
        return remote(
            owed.at[kind], owed.at[kind], back_send.at[kind], back_recv.at[kind], here.ctx_device(1)
        )

    @pl.when(second_core)
    def _():
        def clear(j, carry):
            for kind in range(2):
                extra[kind, j] = jnp.zeros(extra.shape[2:], extra.dtype)
            return carry

        lax.fori_loop(0, groups, clear, 0)

    @pl.when(jnp.logical_not(takes_back))
    def _():
        owed[...] = jnp.zeros_like(owed)

    load.wait()

    @pl.when(rings_prior)
    def _():
        forward(0, 1)

    @pl.when(here.first_core)
    def _():
        for kind in range(2):
            from_sibling(kind).wait_recv()

    forward(1, 1)
    for step in range(2, 5):

        @pl.when(rings_prior)
        def _():
            forward(0, step)

        forward(1, step)

    @pl.when(rings_prior)
    def _():
        for kind in range(2):
            for direction in range(2):
                arrival(0, kind, direction, depth_of(kind, direction)).wait_recv()

            def finish(j, carry):
                handed[kind, j] = last(0, kind, j).astype(handed.dtype)
                return carry

            lax.fori_loop(0, groups, finish, 0)
            back(kind).start()

    for kind in range(2):
        for direction in range(2):
            arrival(1, kind, direction, depth_of(kind, direction)).wait_recv()

    @pl.when(takes_back)
    def _():
        for kind in range(2):
            from_back(kind).wait_recv()

    def finish(j, carry):
        for kind in range(2):
            value = last(1, kind, j) + owed[kind, j].astype(f32)
            total[kind, j] = value.astype(total.dtype)
        return carry

    lax.fori_loop(0, groups, finish, 0)
    dkv_local = pltpu.make_async_copy(*dkv_pair(group, group), home.at[2])
    dkv_local.start()
    for offset in range(1, groups):
        near(1, offset).start()

    dq_local.wait()
    dkv_local.wait()
    for index in range(2):
        for offset in range(1, groups):
            near_arrival(index, offset).wait_recv()
    for index in range(2):
        for offset in range(1, groups):
            near(index, offset).wait_send()
    for kind, direction in RING:
        for step in range(1, depth_of(kind, direction) + 1):
            hop(1, kind, direction, step).wait_send()

    @pl.when(rings_prior)
    def _():
        for kind, direction in RING:
            for step in range(1, depth_of(kind, direction) + 1):
                hop(0, kind, direction, step).wait_send()
        for kind in range(2):
            back(kind).wait_send()

    @pl.when(second_core)
    def _():
        for kind in range(2):
            sibling(kind).wait_send()


def reduce(dq_rows, dkv):
    groups, tok, per_group, size = dq_rows.shape
    members = dkv.shape[3]
    kind = dkv.dtype
    hbm = pl.BlockSpec(memory_space=pl.ANY)
    block = (groups, tok, size)
    return pl.pallas_call(
        lambda *refs: reduce_kernel(lax.axis_size("ctx"), *refs),
        out_shape=(
            jax.ShapeDtypeStruct((tok, groups * per_group, size), kind),
            jax.ShapeDtypeStruct((2, groups, tok, size), kind),
        ),
        in_specs=[hbm] * 2,
        out_specs=(hbm,) * 2,
        scratch_shapes=[
            pltpu.VMEM(dkv.shape, kind),
            pltpu.VMEM((2, groups, members, tok, size), kind),
            pltpu.VMEM((2, 2, 2, 4) + block, kind),
            pltpu.VMEM((2, 2, 2, 4) + block, kind),
            pltpu.VMEM((2,) + block, kind),
            pltpu.VMEM((2,) + block, kind),
            pltpu.VMEM((2,) + block, kind),
            pltpu.SemaphoreType.DMA((2, groups - 1)),
            pltpu.SemaphoreType.DMA((2, groups - 1)),
            pltpu.SemaphoreType.DMA((3,)),
            pltpu.SemaphoreType.DMA((2, 2, 2, 4)),
            pltpu.SemaphoreType.DMA((2, 2, 2, 4)),
            pltpu.SemaphoreType.DMA((2,)),
            pltpu.SemaphoreType.DMA((2,)),
            pltpu.SemaphoreType.DMA((2,)),
            pltpu.SemaphoreType.DMA((2,)),
        ],
        compiler_params=pltpu.CompilerParams(
            collective_id=1, has_side_effects=True, vmem_limit_bytes=32 * 2**20
        ),
    )(dq_rows, dkv)


def per_device(queries, keys, values, outputs, out_grads, log_norms, block_doc):
    tok, heads_all, size = queries.shape
    groups = keys.shape[1]
    per_group = heads_all // groups
    members = lax.axis_size("head") // groups
    chunk_rows = tok * per_group
    span = tok * groups * members
    blocks = span // BLK

    deltas = jnp.sum(out_grads.astype(jnp.float32) * outputs.astype(jnp.float32), axis=-1)
    stats = jnp.stack([log_norms, deltas]).reshape(2, tok, groups, per_group)
    stats = stats.transpose(2, 0, 1, 3).reshape(groups, 2, chunk_rows)
    kv = jnp.stack([keys, values]).transpose(2, 0, 1, 3)
    q_rows, g_rows, kv_all, stats = gather(queries, out_grads, kv, stats, members)

    member = lax.axis_index("head") % members
    per_chunk = members * tok // BLK
    first_block = member * tok // BLK
    base = lax.axis_index("ctx") * blocks
    own = base + first_block + per_chunk * jnp.arange(groups, dtype=jnp.int32)
    docs = block_doc[own]
    start = jnp.sum((block_doc[None, :] < docs[:, None]).astype(jnp.int32), axis=1) - base + blocks
    geom = jnp.stack(
        [blocks + first_block, jnp.int32(per_chunk), (member * tok) % BLK]
    ).astype(jnp.int32)
    rows = (groups, chunk_rows, size)
    dq_rows, dkv = attention(
        geom,
        start,
        q_rows.reshape(rows),
        g_rows.reshape(rows),
        stats[:, 0],
        stats[:, 1],
        kv_all.reshape(2, 2 * span, size),
    )
    query_grads, dkv = reduce(dq_rows.reshape(q_rows.shape), dkv.reshape(kv_all.shape))
    dkv = dkv.transpose(0, 2, 1, 3)
    return (query_grads, dkv[0], dkv[1])


def solution(mesh):
    tokens = P(("ctx", "head"), None, None)
    return jax.shard_map(
        per_device,
        mesh=mesh,
        in_specs=(tokens, tokens, tokens, tokens, tokens, P(("ctx", "head"), None), P()),
        out_specs=(tokens, tokens, tokens),
        check_vma=False,
    )
```

```python
import math
import jax
import jax.numpy as jnp
from jax import lax
from jax.experimental import pallas as pl
from jax.experimental.pallas import tpu as pltpu
from jax.sharding import PartitionSpec as P

BLK = 128
TILE = 512
EXTENTS = (2, 4, 6, 8)
NT = (((1,), (1,)), ((), ()))
NN = (((1,), (0,)), ((), ()))
TN = (((0,), (0,)), ((), ()))


def attention_kernel(
    members, doc_ref, q_ref, g_ref, stat_ref, kv_ref, dq_ref, dkv_ref,
    item_chunk, item_start, item_tail, probs, grads, dkacc, dvacc, dqacc,
):
    chunks, rows, size = q_ref.shape
    heads = 8
    tok = rows // heads
    span = chunks * members * tok
    total_rows = kv_ref.shape[1]
    before = (total_rows - span) // BLK
    base = lax.axis_index("ctx") * (span // BLK)
    at_token = lax.rem(lax.axis_index("head"), members) * tok
    first = at_token // BLK
    stride = members * tok // BLK
    inner = lax.rem(at_token, BLK)
    tile_blocks = TILE // BLK
    scale = size**-0.5
    scale2 = scale * math.log2(math.e)

    def plan(chunk, carry):
        count, floor, begun = carry
        block = base + first + stride * chunk
        doc = doc_ref[block]

        def more(at):
            ahead = jnp.maximum(at - 1, 0)
            return jnp.logical_and(at > floor, doc_ref[ahead] == doc)

        start = lax.while_loop(more, lambda at: at - 1, block)
        start = jnp.where(jnp.logical_and(start == floor, chunk > 0), begun, start)
        full = (block - start) // tile_blocks

        def put(number, carry):
            item_chunk[count + number] = chunk
            item_start[count + number] = start - base + before + number * tile_blocks
            item_tail[count + number] = (number == full).astype(jnp.int32)
            return carry

        lax.fori_loop(0, full + 1, put, 0)
        return count + full + 1, block, start

    count, _, _ = lax.fori_loop(0, chunks, plan, (jnp.int32(0), jnp.int32(0), jnp.int32(0)))

    step = 512

    def clear(index, carry):
        at = pl.ds(pl.multiple_of(index * step, step), step)
        dkacc[at, :] = jnp.zeros((step, size), jnp.float32)
        dvacc[at, :] = jnp.zeros((step, size), jnp.float32)
        return carry

    lax.fori_loop(0, total_rows // step, clear, 0)

    def clear_dq(index, carry):
        dqacc[index] = jnp.zeros(dqacc.shape[1:], jnp.float32)
        return carry

    lax.fori_loop(0, chunks, clear_dq, 0)
    limit = total_rows - TILE

    def where_of(item):
        begin = item_start[item] * BLK
        return pl.multiple_of(jnp.minimum(begin, limit), BLK), begin

    def score(item, slot, masked):
        chunk = item_chunk[item]
        at, begin = where_of(item)
        rows_at = pl.ds(at, TILE)
        q_rows = q_ref[chunk]
        g_rows = g_ref[chunk]
        norm = stat_ref[chunk, pl.ds(0, 1), :] * math.log2(math.e)
        delta = stat_ref[chunk, pl.ds(1, 1), :]
        scores = lax.dot_general(kv_ref[0, rows_at, :], q_rows, NT, preferred_element_type=jnp.float32)
        value = jnp.exp2(scores * scale2 - norm)
        if masked:
            row = lax.broadcasted_iota(jnp.int32, (TILE, rows), 0) + at
            block = before + first + stride * chunk
            token = lax.broadcasted_iota(jnp.int32, (TILE, rows), 1) // heads + (block * BLK + inner)
            value = jnp.where(jnp.logical_and(row <= token, row >= begin), value, 0.0)
        grad = lax.dot_general(kv_ref[1, rows_at, :], g_rows, NT, preferred_element_type=jnp.float32)
        grads[slot][...] = (value * (grad - delta)).astype(jnp.bfloat16)
        probs[slot][...] = value.astype(jnp.bfloat16)

    def collect(item, slot):
        chunk = item_chunk[item]
        at = pl.ds(where_of(item)[0], TILE)
        dvacc[at, :] += lax.dot_general(probs[slot][...], g_ref[chunk], NN, preferred_element_type=jnp.float32)
        dkacc[at, :] += lax.dot_general(grads[slot][...], q_ref[chunk], NN, preferred_element_type=jnp.float32)
        dqacc[chunk] += lax.dot_general(kv_ref[0, at, :], grads[slot][...], TN, preferred_element_type=jnp.float32)

    @pl.when(item_tail[0] == 1)
    def _():
        score(0, 0, True)

    @pl.when(item_tail[0] == 0)
    def _():
        score(0, 0, False)

    def both(item, slot):
        @pl.when(jnp.logical_and(item < count, item_tail[item] == 1))
        def _():
            collect(item - 1, 1 - slot)
            score(item, slot, True)

        @pl.when(jnp.logical_and(item < count, item_tail[item] == 0))
        def _():
            collect(item - 1, 1 - slot)
            score(item, slot, False)

    def pair(index, carry):
        both(2 * index + 1, 1)
        both(2 * index + 2, 0)
        return carry

    lax.fori_loop(0, count // 2, pair, 0)

    @pl.when(count % 2 == 1)
    def _():
        collect(count - 1, 0)

    @pl.when(count % 2 == 0)
    def _():
        collect(count - 1, 1)

    def flush_dq(index, carry):
        dq_ref[index] = (dqacc[index].T * scale).astype(dq_ref.dtype)
        return carry

    lax.fori_loop(0, chunks, flush_dq, 0)

    def flush(index, carry):
        at = pl.ds(pl.multiple_of(index * step, step), step)
        dkv_ref[0, at, :] = (dkacc[at, :] * scale).astype(dkv_ref.dtype)
        dkv_ref[1, at, :] = dvacc[at, :].astype(dkv_ref.dtype)
        return carry

    lax.fori_loop(0, total_rows // step, flush, 0)


def attention(docs, q_rows, g_rows, stats, kv, members):
    chunks, rows, size = q_rows.shape
    long = kv.shape[1]
    items = chunks * (chunks + 1) + 8
    vmem = pl.BlockSpec(memory_space=pltpu.VMEM)
    smem = pl.BlockSpec(memory_space=pltpu.SMEM)
    return pl.pallas_call(
        lambda *refs: attention_kernel(members, *refs[:10], refs[10:12], refs[12:14], *refs[14:]),
        out_shape=(
            jax.ShapeDtypeStruct(q_rows.shape, jnp.bfloat16),
            jax.ShapeDtypeStruct(kv.shape, jnp.bfloat16),
        ),
        in_specs=[smem, vmem, vmem, vmem, vmem],
        out_specs=(vmem, vmem),
        scratch_shapes=[
            pltpu.SMEM((items,), jnp.int32),
            pltpu.SMEM((items,), jnp.int32),
            pltpu.SMEM((items,), jnp.int32),
            pltpu.VMEM((TILE, rows), jnp.bfloat16),
            pltpu.VMEM((TILE, rows), jnp.bfloat16),
            pltpu.VMEM((TILE, rows), jnp.bfloat16),
            pltpu.VMEM((TILE, rows), jnp.bfloat16),
            pltpu.VMEM((long, size), jnp.float32),
            pltpu.VMEM((long, size), jnp.float32),
            pltpu.VMEM((chunks, size, rows), jnp.float32),
        ],
        compiler_params=pltpu.CompilerParams(vmem_limit_bytes=36 * 2**20),
    )(docs, q_rows, g_rows, stats, kv)


def remote(source, target, send_sem, recv_sem, device):
    return pltpu.make_async_remote_copy(
        src_ref=source,
        dst_ref=target,
        send_sem=send_sem,
        recv_sem=recv_sem,
        device_id=device,
        device_id_type=pl.DeviceIdType.MESH,
    )


class Place:
    def __init__(self, groups, members, ranges):
        self.groups, self.members, self.ranges = groups, members, ranges
        self.ctx = lax.axis_index("ctx")
        head = lax.axis_index("head")
        self.group = head // members
        self.member = lax.rem(head, members)
        self.first_core = lax.rem(self.ctx, 2) == 0
        self.has_prior = self.ctx > 0
        self.has_next = self.ctx < ranges - 1

    def of_group(self, offset):
        return lax.rem(self.group + offset + self.groups, self.groups)

    def of_member(self, offset):
        return lax.rem(self.member + offset + self.members, self.members)

    def group_device(self, offset):
        return (self.ctx, self.of_group(offset) * self.members + self.member)

    def ring_device(self, offset):
        return (self.ctx, self.group * self.members + self.of_member(offset))

    def ctx_device(self, offset):
        return (self.ctx + offset, self.group * self.members + self.member)

    def hello(self):
        barrier = pltpu.get_barrier_semaphore()

        def hello(device):
            pl.semaphore_signal(
                barrier, inc=1, device_id=device, device_id_type=pl.DeviceIdType.MESH
            )

        for offset in range(1, self.groups):
            hello(self.group_device(offset))
        hello(self.ring_device(1))
        hello(self.ring_device(-1))

        @pl.when(self.has_prior)
        def _():
            hello(self.ctx_device(-1))

        @pl.when(self.has_next)
        def _():
            hello(self.ctx_device(1))

    def wait_hello(self):
        extra = self.has_prior.astype(jnp.int32) + self.has_next.astype(jnp.int32)
        pl.semaphore_wait(pltpu.get_barrier_semaphore(), self.groups + 1 + extra)


def depth_of(kind, direction):
    return 4 if kind == direction else 3


RING = [(kind, direction) for kind in range(2) for direction in range(2)]


def gather_kernel(
    ranges,
    extent,
    q_in,
    g_in,
    o_in,
    k_in,
    v_in,
    norm_in,
    q_out,
    g_out,
    kv_out,
    stat_out,
    kv_own,
    stat_own,
    wide,
    k_here,
    v_here,
    g_here,
    o_here,
    norm_here,
    load,
    near_send,
    near_recv,
    home,
    ring_send,
    ring_recv,
    ctx_send,
    ctx_recv,
):
    groups, members = q_out.shape[0], kv_out.shape[2]
    here = Place(groups, members, ranges)
    group, member = here.group, here.member
    tok, per_group, size = q_out.shape[1:]
    rows = tok * per_group

    def pieces(owner, origin):
        heads = pl.ds(pl.multiple_of(owner * per_group, per_group), per_group)
        return [
            (kv_own.at[owner], kv_out.at[:, extent + origin, member]),
            (g_in.at[:, heads, :], g_out.at[origin]),
            (q_in.at[:, heads, :], q_out.at[origin]),
            (stat_own.at[owner], stat_out.at[origin]),
        ]

    def home_copy(index):
        source, target = pieces(group, group)[index]
        return pltpu.make_async_copy(source, target, home.at[index])

    loads = [
        pltpu.make_async_copy(source, target, load.at[index])
        for index, (source, target) in enumerate(
            ((k_in, k_here), (v_in, v_here), (norm_in, norm_here), (g_in, g_here), (o_in, o_here))
        )
    ]
    for copy in loads:
        copy.start()
    here.hello()
    for kind, ref in enumerate((k_here, v_here)):
        loads[kind].wait()
        wide[kind] = ref[...].astype(jnp.float32)
        for owner in range(groups):
            kv_own[owner, kind] = wide[kind, :, owner, :].astype(kv_own.dtype)
    home_copy(0).start()
    here.wait_hello()

    def near(index, offset):
        source, target = pieces(here.of_group(offset), group)[index]
        at = (index, offset - 1)
        return remote(source, target, near_send.at[at], near_recv.at[at], here.group_device(offset))

    def near_arrival(index, offset):
        target = pieces(group, here.of_group(-offset))[index][1]
        at = (index, offset - 1)
        return remote(target, target, near_send.at[at], near_recv.at[at], here.group_device(-offset))

    for offset in range(1, groups):
        near(0, offset).start()

    def piece(part, kind, offset):
        chunks = pl.ds(0, extent) if part == 0 else pl.ds(extent, groups)
        return kv_out.at[kind, chunks, here.of_member(offset)]

    def hop(part, kind, direction, step):
        sign = 1 - 2 * direction
        block = piece(part, kind, -sign * (step - 1))
        at = (part, kind, direction, step - 1)
        return remote(block, block, ring_send.at[at], ring_recv.at[at], here.ring_device(sign))

    def arrival(part, kind, direction, step):
        sign = 1 - 2 * direction
        block = piece(part, kind, -sign * step)
        at = (part, kind, direction, step - 1)
        return remote(block, block, ring_send.at[at], ring_recv.at[at], here.ring_device(-sign))

    def onward(kind, offset):
        at = (kind, offset % members)
        end = kv_out.at[kind, pl.ds(groups, extent), here.of_member(offset)]
        target = piece(0, kind, offset)
        return remote(end, target, ctx_send.at[at], ctx_recv.at[at], here.ctx_device(1))

    def from_prior(kind, offset):
        at = (kind, offset % members)
        block = piece(0, kind, offset)
        return remote(block, block, ctx_send.at[at], ctx_recv.at[at], here.ctx_device(-1))

    rings_prior = jnp.logical_and(here.first_core, here.has_prior)
    takes_prior = jnp.logical_not(here.first_core)

    home_copy(0).wait()
    for offset in range(1, groups):
        near_arrival(0, offset).wait_recv()
    for kind, direction in RING:
        hop(1, kind, direction, 1).start()

    @pl.when(here.has_next)
    def _():
        for kind in range(2):
            onward(kind, 0).start()

    for index in range(1, 3):
        home_copy(index).start()
        for offset in range(1, groups):
            near(index, offset).start()

    for copy in loads[2:]:
        copy.wait()
    exact = lax.Precision.HIGHEST
    f32 = jnp.float32
    lane = lax.broadcasted_iota(jnp.int32, (tok, rows), 1)
    pick = (lane // per_group == lax.broadcasted_iota(jnp.int32, (tok, rows), 0)).astype(f32)
    norms = lax.dot_general(norm_here[...], pick, TN, precision=exact, preferred_element_type=f32)
    lane = lax.broadcasted_iota(jnp.int32, norms.shape, 1)
    head = lax.broadcasted_iota(jnp.int32, norms.shape, 0)
    norms = jnp.where(lax.rem(lane, per_group) == lax.rem(head, per_group), norms, 0.0)
    norms = jnp.sum(norms.reshape(groups, per_group, rows), axis=1)
    ones = jnp.ones((8, size), f32)
    for owner in range(groups):
        heads = pl.ds(owner * per_group, per_group)
        product = g_here[:, heads, :].astype(f32) * o_here[:, heads, :].astype(f32)
        delta = lax.dot_general(
            ones, product.reshape(rows, size), NT, precision=exact, preferred_element_type=f32
        )
        stat_own[owner, pl.ds(0, 1), :] = norms[owner : owner + 1]
        stat_own[owner, pl.ds(1, 1), :] = delta[0:1]
    home_copy(3).start()
    for offset in range(1, groups):
        near(3, offset).start()

    def advance(part, step):
        for kind, direction in RING:
            depth = depth_of(kind, direction)
            if step <= depth:
                arrival(part, kind, direction, step).wait_recv()
                if step < depth:
                    hop(part, kind, direction, step + 1).start()
                if part == 1:

                    @pl.when(here.first_core)
                    def _():
                        onward(kind, (2 * direction - 1) * step).start()

    advance(1, 1)

    @pl.when(rings_prior)
    def _():
        for kind in range(2):
            from_prior(kind, 0).wait_recv()
        for kind, direction in RING:
            hop(0, kind, direction, 1).start()

    for step in range(1, 5):
        if step < 4:
            advance(1, step + 1)

        @pl.when(rings_prior)
        def _():
            advance(0, step)

    @pl.when(takes_prior)
    def _():
        for kind in range(2):
            for offset in range(members):
                from_prior(kind, offset).wait_recv()

    for index in range(1, 4):
        home_copy(index).wait()
        for offset in range(1, groups):
            near_arrival(index, offset).wait_recv()

    for index in range(4):
        for offset in range(1, groups):
            near(index, offset).wait_send()

    def ring_sent(part):
        for kind, direction in RING:
            for step in range(1, depth_of(kind, direction) + 1):
                hop(part, kind, direction, step).wait_send()

    ring_sent(1)

    @pl.when(rings_prior)
    def _():
        ring_sent(0)

    @pl.when(here.has_next)
    def _():
        for kind in range(2):
            onward(kind, 0).wait_send()

    @pl.when(here.first_core)
    def _():
        for kind in range(2):
            for offset in range(1, members):
                onward(kind, offset).wait_send()


def gather(extent, queries, out_grads, outputs, keys, values, log_norms, members):
    tok, heads_all, size = queries.shape
    groups = keys.shape[1]
    per_group = heads_all // groups
    half = keys.dtype
    hbm = pl.BlockSpec(memory_space=pltpu.HBM)
    free = pl.BlockSpec(memory_space=pl.ANY)
    rows = jax.ShapeDtypeStruct((groups, tok, per_group, size), half)
    stats = (groups, 2, tok * per_group)
    return pl.pallas_call(
        lambda *refs: gather_kernel(lax.axis_size("ctx"), extent, *refs),
        out_shape=(
            rows,
            rows,
            jax.ShapeDtypeStruct((2, extent + groups, members, tok, size), half),
            jax.ShapeDtypeStruct(stats, jnp.float32),
        ),
        in_specs=[hbm] * 6,
        out_specs=(free,) * 4,
        scratch_shapes=[
            pltpu.VMEM((groups, 2, tok, size), half),
            pltpu.VMEM(stats, jnp.float32),
            pltpu.VMEM((2,) + keys.shape, jnp.float32),
            pltpu.VMEM(keys.shape, half),
            pltpu.VMEM(keys.shape, half),
            pltpu.VMEM(queries.shape, half),
            pltpu.VMEM(queries.shape, half),
            pltpu.VMEM(log_norms.shape, jnp.float32),
            pltpu.SemaphoreType.DMA((5,)),
            pltpu.SemaphoreType.DMA((4, groups - 1)),
            pltpu.SemaphoreType.DMA((4, groups - 1)),
            pltpu.SemaphoreType.DMA((4,)),
            pltpu.SemaphoreType.DMA((2, 2, 2, 4)),
            pltpu.SemaphoreType.DMA((2, 2, 2, 4)),
            pltpu.SemaphoreType.DMA((2, members)),
            pltpu.SemaphoreType.DMA((2, members)),
        ],
        compiler_params=pltpu.CompilerParams(
            collective_id=extent, has_side_effects=True, vmem_limit_bytes=10 * 2**20
        ),
    )(queries, out_grads, outputs, keys, values, log_norms)


def reduce_kernel(
    ranges,
    extent,
    dq_in,
    dkv_in,
    dq_out,
    dk_out,
    dv_out,
    extra,
    got_prior,
    got_own,
    sent_prior,
    sent_own,
    handed,
    owed,
    total,
    landed,
    wide,
    near_send,
    near_recv,
    home,
    ring_send,
    ring_recv,
    ctx_send,
    ctx_recv,
    back_send,
    back_recv,
):
    groups, members = dq_in.shape[0], dkv_in.shape[2]
    here = Place(groups, members, ranges)
    group, member = here.group, here.member
    per_group = dq_in.shape[2]
    f32 = jnp.float32
    got, sent = (got_prior, got_own), (sent_prior, sent_own)
    plain = groups - extent

    def dq_pair(owner, origin):
        heads = pl.ds(pl.multiple_of(origin * per_group, per_group), per_group)
        return dq_in.at[owner], dq_out.at[:, heads, :]

    def dkv_pair(owner, origin):
        return total.at[:, owner], landed.at[:, origin]

    dq_local = pltpu.make_async_copy(*dq_pair(group, group), home.at[0])
    dq_local.start()
    here.hello()
    rings_prior = jnp.logical_and(here.first_core, here.has_prior)
    second_core = jnp.logical_not(here.first_core)
    takes_back = jnp.logical_and(second_core, here.has_next)

    @pl.when(second_core)
    def _():
        def clear(j, carry):
            for kind in range(2):
                extra[kind, j] = jnp.zeros(extra.shape[2:], extra.dtype)
            return carry

        lax.fori_loop(0, extent, clear, 0)

    @pl.when(jnp.logical_not(takes_back))
    def _():
        owed[...] = jnp.zeros_like(owed)

    here.wait_hello()

    def sibling(kind, offset):
        owner = here.of_member(offset)
        at = (kind, offset % members)
        return remote(
            dkv_in.at[kind, pl.ds(0, extent), owner],
            extra.at[kind, :, owner],
            ctx_send.at[at],
            ctx_recv.at[at],
            here.ctx_device(-1),
        )

    def from_sibling(kind, offset):
        at = (kind, offset % members)
        block = extra.at[kind, :, here.of_member(offset)]
        return remote(block, block, ctx_send.at[at], ctx_recv.at[at], here.ctx_device(1))

    def owner_at(kind, direction, step):
        return (1 - 2 * direction) * (depth_of(kind, direction) - step + 1)

    @pl.when(second_core)
    def _():
        for step in range(1, 5):
            for kind, direction in RING:
                if step <= depth_of(kind, direction):
                    sibling(kind, owner_at(kind, direction, step)).start()
        for kind in range(2):
            sibling(kind, 0).start()

    def near(index, offset):
        pair = (dq_pair, dkv_pair)[index]
        source, target = pair(here.of_group(offset), group)
        at = (index, offset - 1)
        return remote(source, target, near_send.at[at], near_recv.at[at], here.group_device(offset))

    def near_arrival(index, offset):
        pair = (dq_pair, dkv_pair)[index]
        target = pair(group, here.of_group(-offset))[1]
        at = (index, offset - 1)
        return remote(target, target, near_send.at[at], near_recv.at[at], here.group_device(-offset))

    def hop(which, kind, direction, step):
        sign = 1 - 2 * direction
        at = (kind, direction, step - 1)
        to = (which,) + at
        source = sent[which].at[at]
        return remote(
            source, got[which].at[at], ring_send.at[to], ring_recv.at[to], here.ring_device(sign)
        )

    def arrival(which, kind, direction, step):
        sign = 1 - 2 * direction
        at = (kind, direction, step - 1)
        to = (which,) + at
        block = got[which].at[at]
        return remote(block, block, ring_send.at[to], ring_recv.at[to], here.ring_device(-sign))

    def each(which, write):
        if which == 0:
            lax.fori_loop(0, extent, lambda j, c: (write(j, False), c)[1], 0)
        else:
            if plain:
                lax.fori_loop(0, plain, lambda j, c: (write(j, False), c)[1], 0)
            lax.fori_loop(plain, groups, lambda j, c: (write(j, True), c)[1], 0)

    def mine(which, kind, j, owner, with_extra):
        value = dkv_in[kind, j + which * extent, owner].astype(f32)
        if with_extra:
            value = value + extra[kind, j - plain, owner].astype(f32)
        return value

    def forward(which, step):
        for kind, direction in RING:
            depth = depth_of(kind, direction)
            if step > depth:
                continue
            offset = owner_at(kind, direction, step)
            owner = here.of_member(offset)
            if which == 1:

                @pl.when(here.first_core)
                def _():
                    from_sibling(kind, offset).wait_recv()

            if step > 1:
                arrival(which, kind, direction, step - 1).wait_recv()

            def write(j, with_extra):
                value = mine(which, kind, j, owner, with_extra)
                if step > 1:
                    value = value + got[which][kind, direction, step - 2, j].astype(f32)
                sent[which][kind, direction, step - 1, j] = value.astype(dkv_in.dtype)

            each(which, write)
            hop(which, kind, direction, step).start()

    def last(which, kind, j, with_extra):
        value = mine(which, kind, j, member, with_extra)
        for direction in range(2):
            depth = depth_of(kind, direction)
            value = value + got[which][kind, direction, depth - 1, j].astype(f32)
        return value

    def back(kind):
        return remote(
            handed.at[kind],
            owed.at[kind],
            back_send.at[kind],
            back_recv.at[kind],
            here.ctx_device(-1),
        )

    def from_back(kind):
        return remote(
            owed.at[kind], owed.at[kind], back_send.at[kind], back_recv.at[kind], here.ctx_device(1)
        )

    def hand_back():
        for kind in range(2):
            for direction in range(2):
                arrival(0, kind, direction, depth_of(kind, direction)).wait_recv()

            def write(j, with_extra):
                handed[kind, j] = last(0, kind, j, with_extra).astype(handed.dtype)

            each(0, write)
            back(kind).start()

    def on_prior(action):
        pl.when(rings_prior)(action)

    on_prior(lambda: forward(0, 1))
    forward(1, 1)
    for offset in range(1, groups):
        near(0, offset).start()
    for step in range(2, 5):
        on_prior(lambda: forward(0, step))
        if step == 4:
            on_prior(hand_back)
        forward(1, step)

    for kind in range(2):
        for direction in range(2):
            arrival(1, kind, direction, depth_of(kind, direction)).wait_recv()

        @pl.when(here.first_core)
        def _():
            from_sibling(kind, 0).wait_recv()

    @pl.when(takes_back)
    def _():
        for kind in range(2):
            from_back(kind).wait_recv()

    for kind in range(2):

        def write(j, with_extra):
            value = last(1, kind, j, with_extra)
            if with_extra:
                value = value + owed[kind, j - plain].astype(f32)
            total[kind, j] = value.astype(total.dtype)

        each(1, write)
    dkv_local = pltpu.make_async_copy(*dkv_pair(group, group), home.at[1])
    dkv_local.start()
    for offset in range(1, groups):
        near(1, offset).start()

    for offset in range(1, groups):
        near(0, offset).wait_send()
        near_arrival(0, offset).wait_recv()
    for kind, direction in RING:
        for step in range(1, depth_of(kind, direction) + 1):
            hop(1, kind, direction, step).wait_send()

    @pl.when(rings_prior)
    def _():
        for kind, direction in RING:
            for step in range(1, depth_of(kind, direction) + 1):
                hop(0, kind, direction, step).wait_send()
        for kind in range(2):
            back(kind).wait_send()

    @pl.when(second_core)
    def _():
        for kind in range(2):
            for offset in range(members):
                sibling(kind, offset).wait_send()

    dq_local.wait()
    dkv_local.wait()
    for offset in range(1, groups):
        near_arrival(1, offset).wait_recv()
    for kind, ref in enumerate((dk_out, dv_out)):
        for owner in range(groups):
            wide[kind, :, owner, :] = landed[kind, owner].astype(f32)
        ref[...] = wide[kind].astype(ref.dtype)
    for offset in range(1, groups):
        near(1, offset).wait_send()


def reduce(extent, dq_rows, dkv):
    groups, tok, per_group, size = dq_rows.shape
    members = dkv.shape[2]
    half = dkv.dtype
    hbm = pl.BlockSpec(memory_space=pl.ANY)
    vmem = pl.BlockSpec(memory_space=pltpu.VMEM)
    whole, end = (groups, tok, size), (extent, tok, size)
    grads = jax.ShapeDtypeStruct((tok, groups, size), half)
    return pl.pallas_call(
        lambda *refs: reduce_kernel(lax.axis_size("ctx"), extent, *refs),
        out_shape=(jax.ShapeDtypeStruct((tok, groups * per_group, size), half), grads, grads),
        in_specs=[hbm, vmem],
        out_specs=(hbm, vmem, vmem),
        scratch_shapes=[
            pltpu.VMEM((2, extent, members, tok, size), half),
            pltpu.VMEM((2, 2, 4) + end, half),
            pltpu.VMEM((2, 2, 4) + whole, half),
            pltpu.VMEM((2, 2, 4) + end, half),
            pltpu.VMEM((2, 2, 4) + whole, half),
            pltpu.VMEM((2,) + end, half),
            pltpu.VMEM((2,) + end, half),
            pltpu.VMEM((2,) + whole, half),
            pltpu.VMEM((2,) + whole, half),
            pltpu.VMEM((2, tok, groups, size), jnp.float32),
            pltpu.SemaphoreType.DMA((2, groups - 1)),
            pltpu.SemaphoreType.DMA((2, groups - 1)),
            pltpu.SemaphoreType.DMA((2,)),
            pltpu.SemaphoreType.DMA((2, 2, 2, 4)),
            pltpu.SemaphoreType.DMA((2, 2, 2, 4)),
            pltpu.SemaphoreType.DMA((2, members)),
            pltpu.SemaphoreType.DMA((2, members)),
            pltpu.SemaphoreType.DMA((2,)),
            pltpu.SemaphoreType.DMA((2,)),
        ],
        compiler_params=pltpu.CompilerParams(
            collective_id=16 + extent, has_side_effects=True, vmem_limit_bytes=28 * 2**20
        ),
    )(dq_rows, dkv)


def reach_kernel(ranges, docs, out):
    length = docs.shape[0] // ranges
    reach = jnp.int32(0)
    for boundary in range(1, ranges):
        at = boundary * length
        doc = docs[at]

        def more(count):
            return jnp.logical_and(count < length, docs[at - 1 - jnp.minimum(count, length - 1)] == doc)

        reach = jnp.maximum(reach, lax.while_loop(more, lambda count: count + 1, jnp.int32(0)))
    out[0] = reach


def per_device(queries, keys, values, outputs, out_grads, log_norms, block_doc):
    tok, heads_all, size = queries.shape
    groups = keys.shape[1]
    per_group = heads_all // groups
    members = lax.axis_size("head") // groups
    ranges = lax.axis_size("ctx")

    def with_extent(extent):
        def run():
            q_rows, g_rows, kv, stats = gather(
                extent, queries, out_grads, outputs, keys, values, log_norms, members
            )
            rows = (groups, tok * per_group, size)
            dq_rows, dkv = attention(
                block_doc,
                q_rows.reshape(rows),
                g_rows.reshape(rows),
                stats,
                kv.reshape(2, -1, size),
                members,
            )
            return reduce(extent, dq_rows.reshape(q_rows.shape), dkv.reshape(kv.shape))

        return run

    if len(EXTENTS) == 1:
        return with_extent(EXTENTS[0])()
    smem = pl.BlockSpec(memory_space=pltpu.SMEM)
    reach = pl.pallas_call(
        lambda *refs: reach_kernel(ranges, *refs),
        out_shape=jax.ShapeDtypeStruct((1,), jnp.int32),
        in_specs=[smem],
        out_specs=smem,
    )(block_doc)[0]
    chunk_blocks = members * tok // BLK
    which = sum((reach > extent * chunk_blocks).astype(jnp.int32) for extent in EXTENTS[:-1])
    return lax.switch(which, [with_extent(extent) for extent in EXTENTS])


def solution(mesh):
    tokens = P(("ctx", "head"), None, None)
    return jax.shard_map(
        per_device,
        mesh=mesh,
        in_specs=(tokens, tokens, tokens, tokens, tokens, P(("ctx", "head"), None), P()),
        out_specs=(tokens, tokens, tokens),
        check_vma=False,
    )
```

```python
import math
import jax
import jax.numpy as jnp
from jax import lax
from jax.experimental import pallas as pl
from jax.experimental.pallas import tpu as pltpu
from jax.sharding import PartitionSpec as P

BLK = 128
TILE = 512
NT = (((1,), (1,)), ((), ()))
NN = (((1,), (0,)), ((), ()))
TN = (((0,), (0,)), ((), ()))


def attention_kernel(
    members, doc_ref, q_ref, g_ref, stat_ref, kv_ref, dq_ref, dkv_ref,
    item_chunk, item_start, item_tail, dkacc, dvacc, dqacc,
):
    chunks, rows, size = q_ref.shape
    heads = 8
    tok = rows // heads
    span = chunks * members * tok
    total_rows = kv_ref.shape[1]
    before = (total_rows - span) // BLK
    base = lax.axis_index("ctx") * (span // BLK)
    at_token = lax.rem(lax.axis_index("head"), members) * tok
    first = at_token // BLK
    stride = members * tok // BLK
    inner = lax.rem(at_token, BLK)
    tile_blocks = TILE // BLK
    scale = size**-0.5
    scale2 = scale * math.log2(math.e)

    def plan(chunk, carry):
        count, floor, begun = carry
        block = base + first + stride * chunk
        doc = doc_ref[block]

        def more(at):
            ahead = jnp.maximum(at - 1, 0)
            return jnp.logical_and(at > floor, doc_ref[ahead] == doc)

        start = lax.while_loop(more, lambda at: at - 1, block)
        start = jnp.where(jnp.logical_and(start == floor, chunk > 0), begun, start)
        full = (block - start) // tile_blocks

        def put(number, carry):
            item_chunk[count + number] = chunk
            item_start[count + number] = start - base + before + number * tile_blocks
            item_tail[count + number] = (number == full).astype(jnp.int32)
            return carry

        lax.fori_loop(0, full + 1, put, 0)
        return count + full + 1, block, start

    count, _, _ = lax.fori_loop(0, chunks, plan, (jnp.int32(0), jnp.int32(0), jnp.int32(0)))

    step = 512

    def clear(index, carry):
        at = pl.ds(pl.multiple_of(index * step, step), step)
        dkacc[at, :] = jnp.zeros((step, size), jnp.float32)
        dvacc[at, :] = jnp.zeros((step, size), jnp.float32)
        return carry

    lax.fori_loop(0, total_rows // step, clear, 0)

    def clear_dq(index, carry):
        dqacc[index] = jnp.zeros(dqacc.shape[1:], jnp.float32)
        return carry

    lax.fori_loop(0, chunks, clear_dq, 0)
    limit = total_rows - TILE

    def where_of(item):
        begin = item_start[item] * BLK
        return pl.multiple_of(jnp.minimum(begin, limit), BLK), begin

    def tile(item, masked):
        chunk = item_chunk[item]
        at, begin = where_of(item)
        rows_at = pl.ds(at, TILE)
        keys = kv_ref[0, rows_at, :]
        q_rows = q_ref[chunk]
        g_rows = g_ref[chunk]
        norm = stat_ref[chunk, pl.ds(0, 1), :] * math.log2(math.e)
        delta = stat_ref[chunk, pl.ds(1, 1), :]
        scores = lax.dot_general(keys, q_rows, NT, preferred_element_type=jnp.float32)
        value = jnp.exp2(scores * scale2 - norm)
        if masked:
            row = lax.broadcasted_iota(jnp.int32, (TILE, rows), 0) + at
            block = before + first + stride * chunk
            token = lax.broadcasted_iota(jnp.int32, (TILE, rows), 1) // heads + (block * BLK + inner)
            value = jnp.where(jnp.logical_and(row <= token, row >= begin), value, 0.0)
        grad = lax.dot_general(
            kv_ref[1, rows_at, :], g_rows, NT, preferred_element_type=jnp.float32
        )
        grads = (value * (grad - delta)).astype(jnp.bfloat16)
        dvacc[rows_at, :] += lax.dot_general(
            value.astype(jnp.bfloat16), g_rows, NN, preferred_element_type=jnp.float32
        )
        dkacc[rows_at, :] += lax.dot_general(grads, q_rows, NN, preferred_element_type=jnp.float32)
        dqacc[chunk] += lax.dot_general(keys, grads, TN, preferred_element_type=jnp.float32)

    def visit(item, carry):
        @pl.when(item_tail[item] == 1)
        def _():
            tile(item, True)

        @pl.when(item_tail[item] == 0)
        def _():
            tile(item, False)

        return carry

    lax.fori_loop(0, count, visit, 0)

    def flush_dq(index, carry):
        dq_ref[index] = (dqacc[index].T * scale).astype(dq_ref.dtype)
        return carry

    lax.fori_loop(0, chunks, flush_dq, 0)

    def flush(index, carry):
        at = pl.ds(pl.multiple_of(index * step, step), step)
        dkv_ref[0, at, :] = (dkacc[at, :] * scale).astype(dkv_ref.dtype)
        dkv_ref[1, at, :] = dvacc[at, :].astype(dkv_ref.dtype)
        return carry

    lax.fori_loop(0, total_rows // step, flush, 0)


def attention(docs, q_rows, g_rows, stats, kv, members):
    chunks, rows, size = q_rows.shape
    long = kv.shape[1]
    items = chunks * (chunks + 1) + 8
    vmem = pl.BlockSpec(memory_space=pltpu.VMEM)
    smem = pl.BlockSpec(memory_space=pltpu.SMEM)
    return pl.pallas_call(
        lambda *refs: attention_kernel(members, *refs),
        out_shape=(
            jax.ShapeDtypeStruct(q_rows.shape, jnp.bfloat16),
            jax.ShapeDtypeStruct(kv.shape, jnp.bfloat16),
        ),
        in_specs=[smem, vmem, vmem, vmem, vmem],
        out_specs=(vmem, vmem),
        scratch_shapes=[
            pltpu.SMEM((items,), jnp.int32),
            pltpu.SMEM((items,), jnp.int32),
            pltpu.SMEM((items,), jnp.int32),
            pltpu.VMEM((long, size), jnp.float32),
            pltpu.VMEM((long, size), jnp.float32),
            pltpu.VMEM((chunks, size, rows), jnp.float32),
        ],
        compiler_params=pltpu.CompilerParams(vmem_limit_bytes=36 * 2**20),
    )(docs, q_rows, g_rows, stats, kv)


def remote(source, target, send_sem, recv_sem, device):
    return pltpu.make_async_remote_copy(
        src_ref=source,
        dst_ref=target,
        send_sem=send_sem,
        recv_sem=recv_sem,
        device_id=device,
        device_id_type=pl.DeviceIdType.MESH,
    )


class Place:
    def __init__(self, groups, members, ranges):
        self.groups, self.members, self.ranges = groups, members, ranges
        self.ctx = lax.axis_index("ctx")
        head = lax.axis_index("head")
        self.group = head // members
        self.member = lax.rem(head, members)
        self.first_core = lax.rem(self.ctx, 2) == 0
        self.has_prior = self.ctx > 0
        self.has_next = self.ctx < ranges - 1

    def of_group(self, offset):
        return lax.rem(self.group + offset + self.groups, self.groups)

    def of_member(self, offset):
        return lax.rem(self.member + offset + self.members, self.members)

    def group_device(self, offset):
        return (self.ctx, self.of_group(offset) * self.members + self.member)

    def ring_device(self, offset):
        return (self.ctx, self.group * self.members + self.of_member(offset))

    def ctx_device(self, offset):
        return (self.ctx + offset, self.group * self.members + self.member)

    def hello(self):
        barrier = pltpu.get_barrier_semaphore()

        def hello(device):
            pl.semaphore_signal(
                barrier, inc=1, device_id=device, device_id_type=pl.DeviceIdType.MESH
            )

        for offset in range(1, self.groups):
            hello(self.group_device(offset))
        hello(self.ring_device(1))
        hello(self.ring_device(-1))

        @pl.when(self.has_prior)
        def _():
            hello(self.ctx_device(-1))

        @pl.when(self.has_next)
        def _():
            hello(self.ctx_device(1))

    def wait_hello(self):
        extra = self.has_prior.astype(jnp.int32) + self.has_next.astype(jnp.int32)
        pl.semaphore_wait(pltpu.get_barrier_semaphore(), self.groups + 1 + extra)


def others(groups, action):
    def step(offset, carry):
        action(offset)
        return carry

    lax.fori_loop(1, groups, step, 0)


def depth_of(kind, direction):
    return 4 if kind == direction else 3


RING = [(kind, direction) for kind in range(2) for direction in range(2)]


def gather_kernel(
    ranges,
    extent,
    q_in,
    g_in,
    o_in,
    k_in,
    v_in,
    norm_in,
    q_out,
    g_out,
    kv_out,
    stat_out,
    kv_own,
    stat_own,
    wide,
    k_here,
    v_here,
    g_here,
    o_here,
    norm_here,
    load,
    near_send,
    near_recv,
    home,
    ring_send,
    ring_recv,
    ctx_send,
    ctx_recv,
):
    groups, members = q_out.shape[0], kv_out.shape[2]
    here = Place(groups, members, ranges)
    group, member = here.group, here.member
    tok, per_group, size = q_out.shape[1:]
    rows = tok * per_group

    def pieces(owner, origin):
        heads = pl.ds(pl.multiple_of(owner * per_group, per_group), per_group)
        return [
            (kv_own.at[owner], kv_out.at[:, extent + origin, member]),
            (g_in.at[:, heads, :], g_out.at[origin]),
            (q_in.at[:, heads, :], q_out.at[origin]),
            (stat_own.at[owner], stat_out.at[origin]),
        ]

    def home_copy(index):
        source, target = pieces(group, group)[index]
        return pltpu.make_async_copy(source, target, home.at[index])

    loads = [
        pltpu.make_async_copy(source, target, load.at[index])
        for index, (source, target) in enumerate(
            ((k_in, k_here), (v_in, v_here), (norm_in, norm_here), (g_in, g_here), (o_in, o_here))
        )
    ]
    for copy in loads:
        copy.start()
    here.hello()
    for kind, ref in enumerate((k_here, v_here)):
        loads[kind].wait()
        wide[kind] = ref[...].astype(jnp.float32)
        for owner in range(groups):
            kv_own[owner, kind] = wide[kind, :, owner, :].astype(kv_own.dtype)
    home_copy(0).start()
    here.wait_hello()

    def near(index, offset):
        source, target = pieces(here.of_group(offset), group)[index]
        at = (index, offset - 1)
        return remote(source, target, near_send.at[at], near_recv.at[at], here.group_device(offset))

    def near_arrival(index, offset):
        target = pieces(group, here.of_group(-offset))[index][1]
        at = (index, offset - 1)
        return remote(target, target, near_send.at[at], near_recv.at[at], here.group_device(-offset))

    others(groups, lambda offset: [near(0, offset).start()])

    def piece(part, kind, offset):
        chunks = pl.ds(0, extent) if part == 0 else pl.ds(extent, groups)
        return kv_out.at[kind, chunks, here.of_member(offset)]

    def hop(part, kind, direction, step):
        sign = 1 - 2 * direction
        block = piece(part, kind, -sign * (step - 1))
        at = (part, kind, direction, step - 1)
        return remote(block, block, ring_send.at[at], ring_recv.at[at], here.ring_device(sign))

    def arrival(part, kind, direction, step):
        sign = 1 - 2 * direction
        block = piece(part, kind, -sign * step)
        at = (part, kind, direction, step - 1)
        return remote(block, block, ring_send.at[at], ring_recv.at[at], here.ring_device(-sign))

    def onward(kind, offset):
        at = (kind, offset % members)
        end = kv_out.at[kind, pl.ds(groups, extent), here.of_member(offset)]
        target = piece(0, kind, offset)
        return remote(end, target, ctx_send.at[at], ctx_recv.at[at], here.ctx_device(1))

    def from_prior(kind, offset):
        at = (kind, offset % members)
        block = piece(0, kind, offset)
        return remote(block, block, ctx_send.at[at], ctx_recv.at[at], here.ctx_device(-1))

    rings_prior = jnp.logical_and(here.first_core, here.has_prior)
    takes_prior = jnp.logical_not(here.first_core)

    home_copy(0).wait()
    others(groups, lambda offset: [near_arrival(0, offset).wait_recv()])
    for kind, direction in RING:
        hop(1, kind, direction, 1).start()

    @pl.when(here.has_next)
    def _():
        for kind in range(2):
            onward(kind, 0).start()

    for index in range(1, 3):
        home_copy(index).start()
        others(groups, lambda offset: [near(index, offset).start()])

    for copy in loads[2:]:
        copy.wait()
    exact = lax.Precision.HIGHEST
    f32 = jnp.float32
    lane = lax.broadcasted_iota(jnp.int32, (tok, rows), 1)
    pick = (lane // per_group == lax.broadcasted_iota(jnp.int32, (tok, rows), 0)).astype(f32)
    norms = lax.dot_general(norm_here[...], pick, TN, precision=exact, preferred_element_type=f32)
    lane = lax.broadcasted_iota(jnp.int32, norms.shape, 1)
    head = lax.broadcasted_iota(jnp.int32, norms.shape, 0)
    norms = jnp.where(lax.rem(lane, per_group) == lax.rem(head, per_group), norms, 0.0)
    norms = jnp.sum(norms.reshape(groups, per_group, rows), axis=1)
    ones = jnp.ones((8, size), f32)
    for owner in range(groups):
        heads = pl.ds(owner * per_group, per_group)
        product = g_here[:, heads, :].astype(f32) * o_here[:, heads, :].astype(f32)
        delta = lax.dot_general(
            ones, product.reshape(rows, size), NT, precision=exact, preferred_element_type=f32
        )
        stat_own[owner, pl.ds(0, 1), :] = norms[owner : owner + 1]
        stat_own[owner, pl.ds(1, 1), :] = delta[0:1]
    home_copy(3).start()
    others(groups, lambda offset: [near(3, offset).start()])

    def advance(part, step):
        for kind, direction in RING:
            depth = depth_of(kind, direction)
            if step <= depth:
                arrival(part, kind, direction, step).wait_recv()
                if step < depth:
                    hop(part, kind, direction, step + 1).start()
                if part == 1:

                    @pl.when(here.first_core)
                    def _():
                        onward(kind, (2 * direction - 1) * step).start()

    @pl.when(rings_prior)
    def _():
        for kind in range(2):
            from_prior(kind, 0).wait_recv()
        for kind, direction in RING:
            hop(0, kind, direction, 1).start()

    for step in range(1, 5):
        advance(1, step)

        @pl.when(rings_prior)
        def _():
            advance(0, step)

    @pl.when(takes_prior)
    def _():
        for kind in range(2):
            for offset in range(members):
                from_prior(kind, offset).wait_recv()

    for index in range(1, 4):
        home_copy(index).wait()
        others(groups, lambda offset: [near_arrival(index, offset).wait_recv()])

    for index in range(4):
        others(groups, lambda offset: [near(index, offset).wait_send()])

    def ring_sent(part):
        for kind, direction in RING:
            for step in range(1, depth_of(kind, direction) + 1):
                hop(part, kind, direction, step).wait_send()

    ring_sent(1)

    @pl.when(rings_prior)
    def _():
        ring_sent(0)

    @pl.when(here.has_next)
    def _():
        for kind in range(2):
            onward(kind, 0).wait_send()

    @pl.when(here.first_core)
    def _():
        for kind in range(2):
            for offset in range(1, members):
                onward(kind, offset).wait_send()


def gather(extent, queries, out_grads, outputs, keys, values, log_norms, members):
    tok, heads_all, size = queries.shape
    groups = keys.shape[1]
    per_group = heads_all // groups
    half = keys.dtype
    hbm = pl.BlockSpec(memory_space=pltpu.HBM)
    free = pl.BlockSpec(memory_space=pl.ANY)
    rows = jax.ShapeDtypeStruct((groups, tok, per_group, size), half)
    stats = (groups, 2, tok * per_group)
    return pl.pallas_call(
        lambda *refs: gather_kernel(lax.axis_size("ctx"), extent, *refs),
        out_shape=(
            rows,
            rows,
            jax.ShapeDtypeStruct((2, extent + groups, members, tok, size), half),
            jax.ShapeDtypeStruct(stats, jnp.float32),
        ),
        in_specs=[hbm] * 6,
        out_specs=(free,) * 4,
        scratch_shapes=[
            pltpu.VMEM((groups, 2, tok, size), half),
            pltpu.VMEM(stats, jnp.float32),
            pltpu.VMEM((2,) + keys.shape, jnp.float32),
            pltpu.VMEM(keys.shape, half),
            pltpu.VMEM(keys.shape, half),
            pltpu.VMEM(queries.shape, half),
            pltpu.VMEM(queries.shape, half),
            pltpu.VMEM(log_norms.shape, jnp.float32),
            pltpu.SemaphoreType.DMA((5,)),
            pltpu.SemaphoreType.DMA((4, groups - 1)),
            pltpu.SemaphoreType.DMA((4, groups - 1)),
            pltpu.SemaphoreType.DMA((4,)),
            pltpu.SemaphoreType.DMA((2, 2, 2, 4)),
            pltpu.SemaphoreType.DMA((2, 2, 2, 4)),
            pltpu.SemaphoreType.DMA((2, members)),
            pltpu.SemaphoreType.DMA((2, members)),
        ],
        compiler_params=pltpu.CompilerParams(
            collective_id=0, has_side_effects=True, vmem_limit_bytes=10 * 2**20
        ),
    )(queries, out_grads, outputs, keys, values, log_norms)


def reduce_kernel(
    ranges,
    extent,
    dq_in,
    dkv_in,
    dq_out,
    dk_out,
    dv_out,
    extra,
    got_prior,
    got_own,
    sent_prior,
    sent_own,
    handed,
    owed,
    total,
    landed,
    wide,
    near_send,
    near_recv,
    home,
    ring_send,
    ring_recv,
    ctx_send,
    ctx_recv,
    back_send,
    back_recv,
):
    groups, members = dq_in.shape[0], dkv_in.shape[2]
    here = Place(groups, members, ranges)
    group, member = here.group, here.member
    per_group = dq_in.shape[2]
    f32 = jnp.float32
    got, sent = (got_prior, got_own), (sent_prior, sent_own)
    plain = groups - extent

    def dq_pair(owner, origin):
        heads = pl.ds(pl.multiple_of(origin * per_group, per_group), per_group)
        return dq_in.at[owner], dq_out.at[:, heads, :]

    def dkv_pair(owner, origin):
        return total.at[:, owner], landed.at[:, origin]

    dq_local = pltpu.make_async_copy(*dq_pair(group, group), home.at[0])
    dq_local.start()
    here.hello()
    rings_prior = jnp.logical_and(here.first_core, here.has_prior)
    second_core = jnp.logical_not(here.first_core)
    takes_back = jnp.logical_and(second_core, here.has_next)

    @pl.when(second_core)
    def _():
        def clear(j, carry):
            for kind in range(2):
                extra[kind, j] = jnp.zeros(extra.shape[2:], extra.dtype)
            return carry

        lax.fori_loop(0, extent, clear, 0)

    @pl.when(jnp.logical_not(takes_back))
    def _():
        owed[...] = jnp.zeros_like(owed)

    here.wait_hello()

    def sibling(kind, offset):
        owner = here.of_member(offset)
        at = (kind, offset % members)
        return remote(
            dkv_in.at[kind, pl.ds(0, extent), owner],
            extra.at[kind, :, owner],
            ctx_send.at[at],
            ctx_recv.at[at],
            here.ctx_device(-1),
        )

    def from_sibling(kind, offset):
        at = (kind, offset % members)
        block = extra.at[kind, :, here.of_member(offset)]
        return remote(block, block, ctx_send.at[at], ctx_recv.at[at], here.ctx_device(1))

    def owner_at(kind, direction, step):
        return (1 - 2 * direction) * (depth_of(kind, direction) - step + 1)

    @pl.when(second_core)
    def _():
        for step in range(1, 5):
            for kind, direction in RING:
                if step <= depth_of(kind, direction):
                    sibling(kind, owner_at(kind, direction, step)).start()
        for kind in range(2):
            sibling(kind, 0).start()

    def near(index, offset):
        pair = (dq_pair, dkv_pair)[index]
        source, target = pair(here.of_group(offset), group)
        at = (index, offset - 1)
        return remote(source, target, near_send.at[at], near_recv.at[at], here.group_device(offset))

    def near_arrival(index, offset):
        pair = (dq_pair, dkv_pair)[index]
        target = pair(group, here.of_group(-offset))[1]
        at = (index, offset - 1)
        return remote(target, target, near_send.at[at], near_recv.at[at], here.group_device(-offset))

    def hop(which, kind, direction, step):
        sign = 1 - 2 * direction
        at = (kind, direction, step - 1)
        to = (which,) + at
        source = sent[which].at[at]
        return remote(
            source, got[which].at[at], ring_send.at[to], ring_recv.at[to], here.ring_device(sign)
        )

    def arrival(which, kind, direction, step):
        sign = 1 - 2 * direction
        at = (kind, direction, step - 1)
        to = (which,) + at
        block = got[which].at[at]
        return remote(block, block, ring_send.at[to], ring_recv.at[to], here.ring_device(-sign))

    def each(which, write):
        if which == 0:
            lax.fori_loop(0, extent, lambda j, c: (write(j, False), c)[1], 0)
        else:
            if plain:
                lax.fori_loop(0, plain, lambda j, c: (write(j, False), c)[1], 0)
            lax.fori_loop(plain, groups, lambda j, c: (write(j, True), c)[1], 0)

    def mine(which, kind, j, owner, with_extra):
        value = dkv_in[kind, j + which * extent, owner].astype(f32)
        if with_extra:
            value = value + extra[kind, j - plain, owner].astype(f32)
        return value

    def forward(which, step):
        for kind, direction in RING:
            depth = depth_of(kind, direction)
            if step > depth:
                continue
            offset = owner_at(kind, direction, step)
            owner = here.of_member(offset)
            if which == 1:

                @pl.when(here.first_core)
                def _():
                    from_sibling(kind, offset).wait_recv()

            if step > 1:
                arrival(which, kind, direction, step - 1).wait_recv()

            def write(j, with_extra):
                value = mine(which, kind, j, owner, with_extra)
                if step > 1:
                    value = value + got[which][kind, direction, step - 2, j].astype(f32)
                sent[which][kind, direction, step - 1, j] = value.astype(dkv_in.dtype)

            each(which, write)
            hop(which, kind, direction, step).start()

    def last(which, kind, j, with_extra):
        value = mine(which, kind, j, member, with_extra)
        for direction in range(2):
            depth = depth_of(kind, direction)
            value = value + got[which][kind, direction, depth - 1, j].astype(f32)
        return value

    def back(kind):
        return remote(
            handed.at[kind],
            owed.at[kind],
            back_send.at[kind],
            back_recv.at[kind],
            here.ctx_device(-1),
        )

    def from_back(kind):
        return remote(
            owed.at[kind], owed.at[kind], back_send.at[kind], back_recv.at[kind], here.ctx_device(1)
        )

    def hand_back():
        for kind in range(2):
            for direction in range(2):
                arrival(0, kind, direction, depth_of(kind, direction)).wait_recv()

            def write(j, with_extra):
                handed[kind, j] = last(0, kind, j, with_extra).astype(handed.dtype)

            each(0, write)
            back(kind).start()

    def on_prior(action):
        pl.when(rings_prior)(action)

    for step in range(1, 4):
        on_prior(lambda: forward(0, step))
    forward(1, 1)
    others(groups, lambda offset: [near(0, offset).start()])
    on_prior(lambda: forward(0, 4))
    forward(1, 2)
    on_prior(hand_back)
    forward(1, 3)
    forward(1, 4)

    for kind in range(2):
        for direction in range(2):
            arrival(1, kind, direction, depth_of(kind, direction)).wait_recv()

        @pl.when(here.first_core)
        def _():
            from_sibling(kind, 0).wait_recv()

    @pl.when(takes_back)
    def _():
        for kind in range(2):
            from_back(kind).wait_recv()

    for kind in range(2):

        def write(j, with_extra):
            value = last(1, kind, j, with_extra)
            if with_extra:
                value = value + owed[kind, j - plain].astype(f32)
            total[kind, j] = value.astype(total.dtype)

        each(1, write)
    dkv_local = pltpu.make_async_copy(*dkv_pair(group, group), home.at[1])
    dkv_local.start()
    others(groups, lambda offset: [near(1, offset).start()])

    others(groups, lambda offset: [near(0, offset).wait_send(), near_arrival(0, offset).wait_recv()])
    for kind, direction in RING:
        for step in range(1, depth_of(kind, direction) + 1):
            hop(1, kind, direction, step).wait_send()

    @pl.when(rings_prior)
    def _():
        for kind, direction in RING:
            for step in range(1, depth_of(kind, direction) + 1):
                hop(0, kind, direction, step).wait_send()
        for kind in range(2):
            back(kind).wait_send()

    @pl.when(second_core)
    def _():
        for kind in range(2):
            for offset in range(members):
                sibling(kind, offset).wait_send()

    dq_local.wait()
    dkv_local.wait()
    others(groups, lambda offset: [near_arrival(1, offset).wait_recv()])
    for kind, ref in enumerate((dk_out, dv_out)):
        for owner in range(groups):
            wide[kind, :, owner, :] = landed[kind, owner].astype(f32)
        ref[...] = wide[kind].astype(ref.dtype)
    others(groups, lambda offset: [near(1, offset).wait_send()])


def reduce(extent, dq_rows, dkv):
    groups, tok, per_group, size = dq_rows.shape
    members = dkv.shape[2]
    half = dkv.dtype
    hbm = pl.BlockSpec(memory_space=pl.ANY)
    vmem = pl.BlockSpec(memory_space=pltpu.VMEM)
    whole, end = (groups, tok, size), (extent, tok, size)
    grads = jax.ShapeDtypeStruct((tok, groups, size), half)
    return pl.pallas_call(
        lambda *refs: reduce_kernel(lax.axis_size("ctx"), extent, *refs),
        out_shape=(jax.ShapeDtypeStruct((tok, groups * per_group, size), half), grads, grads),
        in_specs=[hbm, vmem],
        out_specs=(hbm, vmem, vmem),
        scratch_shapes=[
            pltpu.VMEM((2, extent, members, tok, size), half),
            pltpu.VMEM((2, 2, 4) + end, half),
            pltpu.VMEM((2, 2, 4) + whole, half),
            pltpu.VMEM((2, 2, 4) + end, half),
            pltpu.VMEM((2, 2, 4) + whole, half),
            pltpu.VMEM((2,) + end, half),
            pltpu.VMEM((2,) + end, half),
            pltpu.VMEM((2,) + whole, half),
            pltpu.VMEM((2,) + whole, half),
            pltpu.VMEM((2, tok, groups, size), jnp.float32),
            pltpu.SemaphoreType.DMA((2, groups - 1)),
            pltpu.SemaphoreType.DMA((2, groups - 1)),
            pltpu.SemaphoreType.DMA((2,)),
            pltpu.SemaphoreType.DMA((2, 2, 2, 4)),
            pltpu.SemaphoreType.DMA((2, 2, 2, 4)),
            pltpu.SemaphoreType.DMA((2, members)),
            pltpu.SemaphoreType.DMA((2, members)),
            pltpu.SemaphoreType.DMA((2,)),
            pltpu.SemaphoreType.DMA((2,)),
        ],
        compiler_params=pltpu.CompilerParams(
            collective_id=1, has_side_effects=True, vmem_limit_bytes=28 * 2**20
        ),
    )(dq_rows, dkv)


def per_device(queries, keys, values, outputs, out_grads, log_norms, block_doc):
    tok, heads_all, size = queries.shape
    groups = keys.shape[1]
    per_group = heads_all // groups
    members = lax.axis_size("head") // groups
    extent = groups
    there = [
        pltpu.with_memory_space_constraint(array, pltpu.HBM)
        for array in (queries, out_grads, outputs, keys, values, log_norms)
    ]
    q_rows, g_rows, kv, stats = gather(extent, *there, members)
    rows = (groups, tok * per_group, size)
    dq_rows, dkv = attention(
        block_doc,
        q_rows.reshape(rows),
        g_rows.reshape(rows),
        stats,
        kv.reshape(2, -1, size),
        members,
    )
    return reduce(extent, dq_rows.reshape(q_rows.shape), dkv.reshape(kv.shape))


def solution(mesh):
    tokens = P(("ctx", "head"), None, None)
    return jax.shard_map(
        per_device,
        mesh=mesh,
        in_specs=(tokens, tokens, tokens, tokens, tokens, P(("ctx", "head"), None), P()),
        out_specs=(tokens, tokens, tokens),
        check_vma=False,
    )
```

```python
import math
import jax
import jax.numpy as jnp
from jax import lax
from jax.experimental import pallas as pl
from jax.experimental.pallas import tpu as pltpu
from jax.sharding import PartitionSpec as P

BLK = 128
TILE = 512
NT = (((1,), (1,)), ((), ()))
NN = (((1,), (0,)), ((), ()))
TN = (((0,), (0,)), ((), ()))


def attention_kernel(
    members, doc_ref, q_ref, g_ref, stat_ref, kv_ref, dq_ref, dkv_ref,
    item_chunk, item_start, item_tail, dkacc, dvacc, dqacc,
):
    chunks, rows, size = q_ref.shape
    heads = 8
    tok = rows // heads
    span = chunks * members * tok
    total_rows = kv_ref.shape[1]
    before = (total_rows - span) // BLK
    base = lax.axis_index("ctx") * (span // BLK)
    at_token = lax.rem(lax.axis_index("head"), members) * tok
    first = at_token // BLK
    stride = members * tok // BLK
    inner = lax.rem(at_token, BLK)
    tile_blocks = TILE // BLK
    scale = size**-0.5
    scale2 = scale * math.log2(math.e)

    def plan(chunk, carry):
        count, floor, begun = carry
        block = base + first + stride * chunk
        doc = doc_ref[block]

        def more(at):
            ahead = jnp.maximum(at - 1, 0)
            return jnp.logical_and(at > floor, doc_ref[ahead] == doc)

        start = lax.while_loop(more, lambda at: at - 1, block)
        start = jnp.where(jnp.logical_and(start == floor, chunk > 0), begun, start)
        full = (block - start) // tile_blocks

        def put(number, carry):
            item_chunk[count + number] = chunk
            item_start[count + number] = start - base + before + number * tile_blocks
            item_tail[count + number] = (number == full).astype(jnp.int32)
            return carry

        lax.fori_loop(0, full + 1, put, 0)
        return count + full + 1, block, start

    count, _, _ = lax.fori_loop(0, chunks, plan, (jnp.int32(0), jnp.int32(0), jnp.int32(0)))

    step = 512
    touched = item_start[0] * BLK // step

    def clear(index, carry):
        at = pl.ds(pl.multiple_of(index * step, step), step)
        dkacc[at, :] = jnp.zeros((step, size), jnp.float32)
        dvacc[at, :] = jnp.zeros((step, size), jnp.float32)
        return carry

    lax.fori_loop(touched, total_rows // step, clear, 0)

    def clear_dq(index, carry):
        dqacc[index] = jnp.zeros(dqacc.shape[1:], jnp.float32)
        return carry

    lax.fori_loop(0, chunks, clear_dq, 0)
    limit = total_rows - TILE

    def where_of(item):
        begin = item_start[item] * BLK
        return pl.multiple_of(jnp.minimum(begin, limit), BLK), begin

    def tile(item, masked):
        chunk = item_chunk[item]
        at, begin = where_of(item)
        rows_at = pl.ds(at, TILE)
        keys = kv_ref[0, rows_at, :]
        q_rows = q_ref[chunk]
        g_rows = g_ref[chunk]
        norm = stat_ref[chunk, pl.ds(0, 1), :] * math.log2(math.e)
        delta = stat_ref[chunk, pl.ds(1, 1), :]
        scores = lax.dot_general(keys, q_rows, NT, preferred_element_type=jnp.float32)
        value = jnp.exp2(scores * scale2 - norm)
        if masked:
            row = lax.broadcasted_iota(jnp.int32, (TILE, rows), 0) + at
            block = before + first + stride * chunk
            token = lax.broadcasted_iota(jnp.int32, (TILE, rows), 1) // heads + (block * BLK + inner)
            value = jnp.where(jnp.logical_and(row <= token, row >= begin), value, 0.0)
        grad = lax.dot_general(
            kv_ref[1, rows_at, :], g_rows, NT, preferred_element_type=jnp.float32
        )
        grads = (value * (grad - delta)).astype(jnp.bfloat16)
        dvacc[rows_at, :] += lax.dot_general(
            value.astype(jnp.bfloat16), g_rows, NN, preferred_element_type=jnp.float32
        )
        dkacc[rows_at, :] += lax.dot_general(grads, q_rows, NN, preferred_element_type=jnp.float32)
        dqacc[chunk] += lax.dot_general(keys, grads, TN, preferred_element_type=jnp.float32)

    def visit(item, carry):
        @pl.when(item_tail[item] == 1)
        def _():
            tile(item, True)

        @pl.when(item_tail[item] == 0)
        def _():
            tile(item, False)

        return carry

    lax.fori_loop(0, count, visit, 0)

    def flush_dq(index, carry):
        dq_ref[index] = (dqacc[index].T * scale).astype(dq_ref.dtype)
        return carry

    lax.fori_loop(0, chunks, flush_dq, 0)

    def flush(index, carry):
        at = pl.ds(pl.multiple_of(index * step, step), step)
        dkv_ref[0, at, :] = (dkacc[at, :] * scale).astype(dkv_ref.dtype)
        dkv_ref[1, at, :] = dvacc[at, :].astype(dkv_ref.dtype)
        return carry

    def blank(index, carry):
        at = pl.ds(pl.multiple_of(index * step, step), step)
        for kind in range(2):
            dkv_ref[kind, at, :] = jnp.zeros((step, size), dkv_ref.dtype)
        return carry

    lax.fori_loop(0, touched, blank, 0)
    lax.fori_loop(touched, total_rows // step, flush, 0)


def attention(docs, q_rows, g_rows, stats, kv, members):
    chunks, rows, size = q_rows.shape
    long = kv.shape[1]
    items = chunks * (chunks + 1) + 8
    vmem = pl.BlockSpec(memory_space=pltpu.VMEM)
    smem = pl.BlockSpec(memory_space=pltpu.SMEM)
    return pl.pallas_call(
        lambda *refs: attention_kernel(members, *refs),
        out_shape=(
            jax.ShapeDtypeStruct(q_rows.shape, jnp.bfloat16),
            jax.ShapeDtypeStruct(kv.shape, jnp.bfloat16),
        ),
        in_specs=[smem, vmem, vmem, vmem, vmem],
        out_specs=(vmem, vmem),
        scratch_shapes=[
            pltpu.SMEM((items,), jnp.int32),
            pltpu.SMEM((items,), jnp.int32),
            pltpu.SMEM((items,), jnp.int32),
            pltpu.VMEM((long, size), jnp.float32),
            pltpu.VMEM((long, size), jnp.float32),
            pltpu.VMEM((chunks, size, rows), jnp.float32),
        ],
        compiler_params=pltpu.CompilerParams(vmem_limit_bytes=36 * 2**20),
    )(docs, q_rows, g_rows, stats, kv)


def remote(source, target, send_sem, recv_sem, device):
    return pltpu.make_async_remote_copy(
        src_ref=source,
        dst_ref=target,
        send_sem=send_sem,
        recv_sem=recv_sem,
        device_id=device,
        device_id_type=pl.DeviceIdType.MESH,
    )


class Place:
    def __init__(self, groups, members, ranges):
        self.groups, self.members, self.ranges = groups, members, ranges
        self.ctx = lax.axis_index("ctx")
        head = lax.axis_index("head")
        self.group = head // members
        self.member = lax.rem(head, members)
        self.first_core = lax.rem(self.ctx, 2) == 0
        self.has_prior = self.ctx > 0
        self.has_next = self.ctx < ranges - 1

    def of_group(self, offset):
        return lax.rem(self.group + offset + self.groups, self.groups)

    def of_member(self, offset):
        return lax.rem(self.member + offset + self.members, self.members)

    def group_device(self, offset):
        return (self.ctx, self.of_group(offset) * self.members + self.member)

    def ring_device(self, offset):
        return (self.ctx, self.group * self.members + self.of_member(offset))

    def ctx_device(self, offset):
        return (self.ctx + offset, self.group * self.members + self.member)

    def hello(self):
        barrier = pltpu.get_barrier_semaphore()

        def hello(device):
            pl.semaphore_signal(
                barrier, inc=1, device_id=device, device_id_type=pl.DeviceIdType.MESH
            )

        for offset in range(1, self.groups):
            hello(self.group_device(offset))
        hello(self.ring_device(1))
        hello(self.ring_device(-1))

        @pl.when(self.has_prior)
        def _():
            hello(self.ctx_device(-1))

        @pl.when(self.has_next)
        def _():
            hello(self.ctx_device(1))

    def wait_hello(self):
        extra = self.has_prior.astype(jnp.int32) + self.has_next.astype(jnp.int32)
        pl.semaphore_wait(pltpu.get_barrier_semaphore(), self.groups + 1 + extra)


def others(groups, action):
    def step(offset, carry):
        action(offset)
        return carry

    lax.fori_loop(1, groups, step, 0)


def depth_of(kind, direction):
    return 4 if kind == direction else 3


RING = [(kind, direction) for kind in range(2) for direction in range(2)]


def gather_kernel(
    ranges,
    extent,
    q_in,
    g_in,
    o_in,
    k_in,
    v_in,
    norm_in,
    q_out,
    g_out,
    kv_out,
    stat_out,
    kv_own,
    stat_own,
    wide,
    k_here,
    v_here,
    g_here,
    o_here,
    norm_here,
    load,
    near_send,
    near_recv,
    home,
    ring_send,
    ring_recv,
    ctx_send,
    ctx_recv,
):
    groups, members = q_out.shape[0], kv_out.shape[2]
    here = Place(groups, members, ranges)
    group, member = here.group, here.member
    tok, per_group, size = q_out.shape[1:]
    rows = tok * per_group

    def pieces(owner, origin):
        heads = pl.ds(pl.multiple_of(owner * per_group, per_group), per_group)
        return [
            (kv_own.at[owner], kv_out.at[:, extent + origin, member]),
            (g_in.at[:, heads, :], g_out.at[origin]),
            (q_in.at[:, heads, :], q_out.at[origin]),
            (stat_own.at[owner], stat_out.at[origin]),
        ]

    def home_copy(index):
        source, target = pieces(group, group)[index]
        return pltpu.make_async_copy(source, target, home.at[index])

    loads = [
        pltpu.make_async_copy(source, target, load.at[index])
        for index, (source, target) in enumerate(
            ((k_in, k_here), (v_in, v_here), (norm_in, norm_here), (g_in, g_here), (o_in, o_here))
        )
    ]
    for copy in loads:
        copy.start()
    here.hello()
    for kind, ref in enumerate((k_here, v_here)):
        loads[kind].wait()
        wide[kind] = ref[...].astype(jnp.float32)
        for owner in range(groups):
            kv_own[owner, kind] = wide[kind, :, owner, :].astype(kv_own.dtype)
    home_copy(0).start()
    here.wait_hello()

    def near(index, offset):
        source, target = pieces(here.of_group(offset), group)[index]
        at = (index, offset - 1)
        return remote(source, target, near_send.at[at], near_recv.at[at], here.group_device(offset))

    def near_arrival(index, offset):
        target = pieces(group, here.of_group(-offset))[index][1]
        at = (index, offset - 1)
        return remote(target, target, near_send.at[at], near_recv.at[at], here.group_device(-offset))

    others(groups, lambda offset: [near(0, offset).start()])

    def piece(part, kind, offset):
        chunks = pl.ds(0, extent) if part == 0 else pl.ds(extent, groups)
        return kv_out.at[kind, chunks, here.of_member(offset)]

    def hop(part, kind, direction, step):
        sign = 1 - 2 * direction
        block = piece(part, kind, -sign * (step - 1))
        at = (part, kind, direction, step - 1)
        return remote(block, block, ring_send.at[at], ring_recv.at[at], here.ring_device(sign))

    def arrival(part, kind, direction, step):
        sign = 1 - 2 * direction
        block = piece(part, kind, -sign * step)
        at = (part, kind, direction, step - 1)
        return remote(block, block, ring_send.at[at], ring_recv.at[at], here.ring_device(-sign))

    def onward(kind, offset):
        at = (kind, offset % members)
        end = kv_out.at[kind, pl.ds(groups, extent), here.of_member(offset)]
        target = piece(0, kind, offset)
        return remote(end, target, ctx_send.at[at], ctx_recv.at[at], here.ctx_device(1))

    def from_prior(kind, offset):
        at = (kind, offset % members)
        block = piece(0, kind, offset)
        return remote(block, block, ctx_send.at[at], ctx_recv.at[at], here.ctx_device(-1))

    rings_prior = jnp.logical_and(here.first_core, here.has_prior)
    takes_prior = jnp.logical_not(here.first_core)

    home_copy(0).wait()
    others(groups, lambda offset: [near_arrival(0, offset).wait_recv()])
    for kind, direction in RING:
        hop(1, kind, direction, 1).start()

    @pl.when(here.has_next)
    def _():
        for kind in range(2):
            onward(kind, 0).start()

    for index in range(1, 3):
        home_copy(index).start()
        others(groups, lambda offset: [near(index, offset).start()])

    for copy in loads[2:]:
        copy.wait()
    exact = lax.Precision.HIGHEST
    f32 = jnp.float32
    lane = lax.broadcasted_iota(jnp.int32, (tok, rows), 1)
    pick = (lane // per_group == lax.broadcasted_iota(jnp.int32, (tok, rows), 0)).astype(f32)
    norms = lax.dot_general(norm_here[...], pick, TN, precision=exact, preferred_element_type=f32)
    lane = lax.broadcasted_iota(jnp.int32, norms.shape, 1)
    head = lax.broadcasted_iota(jnp.int32, norms.shape, 0)
    norms = jnp.where(lax.rem(lane, per_group) == lax.rem(head, per_group), norms, 0.0)
    norms = jnp.sum(norms.reshape(groups, per_group, rows), axis=1)
    ones = jnp.ones((8, size), f32)
    for owner in range(groups):
        heads = pl.ds(owner * per_group, per_group)
        product = g_here[:, heads, :].astype(f32) * o_here[:, heads, :].astype(f32)
        delta = lax.dot_general(
            ones, product.reshape(rows, size), NT, precision=exact, preferred_element_type=f32
        )
        stat_own[owner, pl.ds(0, 1), :] = norms[owner : owner + 1]
        stat_own[owner, pl.ds(1, 1), :] = delta[0:1]
    home_copy(3).start()
    others(groups, lambda offset: [near(3, offset).start()])

    def advance(part, step):
        for kind, direction in RING:
            depth = depth_of(kind, direction)
            if step <= depth:
                arrival(part, kind, direction, step).wait_recv()
                if step < depth:
                    hop(part, kind, direction, step + 1).start()
                if part == 1:

                    @pl.when(here.first_core)
                    def _():
                        onward(kind, (2 * direction - 1) * step).start()

    @pl.when(rings_prior)
    def _():
        for kind in range(2):
            from_prior(kind, 0).wait_recv()
        for kind, direction in RING:
            hop(0, kind, direction, 1).start()

    for step in range(1, 5):
        advance(1, step)

        @pl.when(rings_prior)
        def _():
            advance(0, step)

    @pl.when(takes_prior)
    def _():
        for kind in range(2):
            for offset in range(members):
                from_prior(kind, offset).wait_recv()

    for index in range(1, 4):
        home_copy(index).wait()
        others(groups, lambda offset: [near_arrival(index, offset).wait_recv()])

    for index in range(4):
        others(groups, lambda offset: [near(index, offset).wait_send()])

    def ring_sent(part):
        for kind, direction in RING:
            for step in range(1, depth_of(kind, direction) + 1):
                hop(part, kind, direction, step).wait_send()

    ring_sent(1)

    @pl.when(rings_prior)
    def _():
        ring_sent(0)

    @pl.when(here.has_next)
    def _():
        for kind in range(2):
            onward(kind, 0).wait_send()

    @pl.when(here.first_core)
    def _():
        for kind in range(2):
            for offset in range(1, members):
                onward(kind, offset).wait_send()


def gather(extent, queries, out_grads, outputs, keys, values, log_norms, members):
    tok, heads_all, size = queries.shape
    groups = keys.shape[1]
    per_group = heads_all // groups
    half = keys.dtype
    hbm = pl.BlockSpec(memory_space=pltpu.HBM)
    free = pl.BlockSpec(memory_space=pl.ANY)
    rows = jax.ShapeDtypeStruct((groups, tok, per_group, size), half)
    stats = (groups, 2, tok * per_group)
    return pl.pallas_call(
        lambda *refs: gather_kernel(lax.axis_size("ctx"), extent, *refs),
        out_shape=(
            rows,
            rows,
            jax.ShapeDtypeStruct((2, extent + groups, members, tok, size), half),
            jax.ShapeDtypeStruct(stats, jnp.float32),
        ),
        in_specs=[hbm] * 6,
        out_specs=(free,) * 4,
        scratch_shapes=[
            pltpu.VMEM((groups, 2, tok, size), half),
            pltpu.VMEM(stats, jnp.float32),
            pltpu.VMEM((2,) + keys.shape, jnp.float32),
            pltpu.VMEM(keys.shape, half),
            pltpu.VMEM(keys.shape, half),
            pltpu.VMEM(queries.shape, half),
            pltpu.VMEM(queries.shape, half),
            pltpu.VMEM(log_norms.shape, jnp.float32),
            pltpu.SemaphoreType.DMA((5,)),
            pltpu.SemaphoreType.DMA((4, groups - 1)),
            pltpu.SemaphoreType.DMA((4, groups - 1)),
            pltpu.SemaphoreType.DMA((4,)),
            pltpu.SemaphoreType.DMA((2, 2, 2, 4)),
            pltpu.SemaphoreType.DMA((2, 2, 2, 4)),
            pltpu.SemaphoreType.DMA((2, members)),
            pltpu.SemaphoreType.DMA((2, members)),
        ],
        compiler_params=pltpu.CompilerParams(
            collective_id=0, has_side_effects=True, vmem_limit_bytes=10 * 2**20
        ),
    )(queries, out_grads, outputs, keys, values, log_norms)


def reduce_kernel(
    ranges,
    extent,
    dq_in,
    dkv_in,
    dq_out,
    dk_out,
    dv_out,
    extra,
    got_prior,
    got_own,
    sent_prior,
    sent_own,
    handed,
    owed,
    total,
    landed,
    wide,
    near_send,
    near_recv,
    home,
    ring_send,
    ring_recv,
    ctx_send,
    ctx_recv,
    back_send,
    back_recv,
):
    groups, members = dq_in.shape[0], dkv_in.shape[2]
    here = Place(groups, members, ranges)
    group, member = here.group, here.member
    per_group = dq_in.shape[2]
    f32 = jnp.float32
    got, sent = (got_prior, got_own), (sent_prior, sent_own)
    plain = groups - extent

    def dq_pair(owner, origin):
        heads = pl.ds(pl.multiple_of(origin * per_group, per_group), per_group)
        return dq_in.at[owner], dq_out.at[:, heads, :]

    def dkv_pair(owner, origin):
        return total.at[:, owner], landed.at[:, origin]

    dq_local = pltpu.make_async_copy(*dq_pair(group, group), home.at[0])
    dq_local.start()
    here.hello()
    rings_prior = jnp.logical_and(here.first_core, here.has_prior)
    second_core = jnp.logical_not(here.first_core)
    takes_back = jnp.logical_and(second_core, here.has_next)

    @pl.when(second_core)
    def _():
        def clear(j, carry):
            for kind in range(2):
                extra[kind, j] = jnp.zeros(extra.shape[2:], extra.dtype)
            return carry

        lax.fori_loop(0, extent, clear, 0)

    @pl.when(jnp.logical_not(takes_back))
    def _():
        owed[...] = jnp.zeros_like(owed)

    here.wait_hello()

    def sibling(kind, offset):
        owner = here.of_member(offset)
        at = (kind, offset % members)
        return remote(
            dkv_in.at[kind, pl.ds(0, extent), owner],
            extra.at[kind, :, owner],
            ctx_send.at[at],
            ctx_recv.at[at],
            here.ctx_device(-1),
        )

    def from_sibling(kind, offset):
        at = (kind, offset % members)
        block = extra.at[kind, :, here.of_member(offset)]
        return remote(block, block, ctx_send.at[at], ctx_recv.at[at], here.ctx_device(1))

    def owner_at(kind, direction, step):
        return (1 - 2 * direction) * (depth_of(kind, direction) - step + 1)

    @pl.when(second_core)
    def _():
        for step in range(1, 5):
            for kind, direction in RING:
                if step <= depth_of(kind, direction):
                    sibling(kind, owner_at(kind, direction, step)).start()
        for kind in range(2):
            sibling(kind, 0).start()

    def near(index, offset):
        pair = (dq_pair, dkv_pair)[index]
        source, target = pair(here.of_group(offset), group)
        at = (index, offset - 1)
        return remote(source, target, near_send.at[at], near_recv.at[at], here.group_device(offset))

    def near_arrival(index, offset):
        pair = (dq_pair, dkv_pair)[index]
        target = pair(group, here.of_group(-offset))[1]
        at = (index, offset - 1)
        return remote(target, target, near_send.at[at], near_recv.at[at], here.group_device(-offset))

    def hop(which, kind, direction, step):
        sign = 1 - 2 * direction
        at = (kind, direction, step - 1)
        to = (which,) + at
        source = sent[which].at[at]
        return remote(
            source, got[which].at[at], ring_send.at[to], ring_recv.at[to], here.ring_device(sign)
        )

    def arrival(which, kind, direction, step):
        sign = 1 - 2 * direction
        at = (kind, direction, step - 1)
        to = (which,) + at
        block = got[which].at[at]
        return remote(block, block, ring_send.at[to], ring_recv.at[to], here.ring_device(-sign))

    def each(which, write):
        if which == 0:
            lax.fori_loop(0, extent, lambda j, c: (write(j, False), c)[1], 0)
        else:
            if plain:
                lax.fori_loop(0, plain, lambda j, c: (write(j, False), c)[1], 0)
            lax.fori_loop(plain, groups, lambda j, c: (write(j, True), c)[1], 0)

    def mine(which, kind, j, owner, with_extra):
        value = dkv_in[kind, j + which * extent, owner].astype(f32)
        if with_extra:
            value = value + extra[kind, j - plain, owner].astype(f32)
        return value

    def forward(which, step):
        for kind, direction in RING:
            depth = depth_of(kind, direction)
            if step > depth:
                continue
            offset = owner_at(kind, direction, step)
            owner = here.of_member(offset)
            if which == 1:

                @pl.when(here.first_core)
                def _():
                    from_sibling(kind, offset).wait_recv()

            if step > 1:
                arrival(which, kind, direction, step - 1).wait_recv()

            def write(j, with_extra):
                value = mine(which, kind, j, owner, with_extra)
                if step > 1:
                    value = value + got[which][kind, direction, step - 2, j].astype(f32)
                sent[which][kind, direction, step - 1, j] = value.astype(dkv_in.dtype)

            each(which, write)
            hop(which, kind, direction, step).start()

    def last(which, kind, j, with_extra):
        value = mine(which, kind, j, member, with_extra)
        for direction in range(2):
            depth = depth_of(kind, direction)
            value = value + got[which][kind, direction, depth - 1, j].astype(f32)
        return value

    def back(kind):
        return remote(
            handed.at[kind],
            owed.at[kind],
            back_send.at[kind],
            back_recv.at[kind],
            here.ctx_device(-1),
        )

    def from_back(kind):
        return remote(
            owed.at[kind], owed.at[kind], back_send.at[kind], back_recv.at[kind], here.ctx_device(1)
        )

    def hand_back():
        for kind in range(2):
            for direction in range(2):
                arrival(0, kind, direction, depth_of(kind, direction)).wait_recv()

            def write(j, with_extra):
                handed[kind, j] = last(0, kind, j, with_extra).astype(handed.dtype)

            each(0, write)
            back(kind).start()

    def on_prior(action):
        pl.when(rings_prior)(action)

    for step in range(1, 4):
        on_prior(lambda: forward(0, step))
    forward(1, 1)
    others(groups, lambda offset: [near(0, offset).start()])
    on_prior(lambda: forward(0, 4))
    forward(1, 2)
    on_prior(hand_back)
    forward(1, 3)
    forward(1, 4)

    for kind in range(2):
        for direction in range(2):
            arrival(1, kind, direction, depth_of(kind, direction)).wait_recv()

        @pl.when(here.first_core)
        def _():
            from_sibling(kind, 0).wait_recv()

    @pl.when(takes_back)
    def _():
        for kind in range(2):
            from_back(kind).wait_recv()

    for kind in range(2):

        def write(j, with_extra):
            value = last(1, kind, j, with_extra)
            if with_extra:
                value = value + owed[kind, j - plain].astype(f32)
            total[kind, j] = value.astype(total.dtype)

        each(1, write)
    dkv_local = pltpu.make_async_copy(*dkv_pair(group, group), home.at[1])
    dkv_local.start()
    others(groups, lambda offset: [near(1, offset).start()])

    others(groups, lambda offset: [near(0, offset).wait_send(), near_arrival(0, offset).wait_recv()])
    for kind, direction in RING:
        for step in range(1, depth_of(kind, direction) + 1):
            hop(1, kind, direction, step).wait_send()

    @pl.when(rings_prior)
    def _():
        for kind, direction in RING:
            for step in range(1, depth_of(kind, direction) + 1):
                hop(0, kind, direction, step).wait_send()
        for kind in range(2):
            back(kind).wait_send()

    @pl.when(second_core)
    def _():
        for kind in range(2):
            for offset in range(members):
                sibling(kind, offset).wait_send()

    dq_local.wait()
    dkv_local.wait()
    others(groups, lambda offset: [near_arrival(1, offset).wait_recv()])
    for kind, ref in enumerate((dk_out, dv_out)):
        for owner in range(groups):
            wide[kind, :, owner, :] = landed[kind, owner].astype(f32)
        ref[...] = wide[kind].astype(ref.dtype)
    others(groups, lambda offset: [near(1, offset).wait_send()])


def reduce(extent, dq_rows, dkv):
    groups, tok, per_group, size = dq_rows.shape
    members = dkv.shape[2]
    half = dkv.dtype
    hbm = pl.BlockSpec(memory_space=pl.ANY)
    vmem = pl.BlockSpec(memory_space=pltpu.VMEM)
    whole, end = (groups, tok, size), (extent, tok, size)
    grads = jax.ShapeDtypeStruct((tok, groups, size), half)
    return pl.pallas_call(
        lambda *refs: reduce_kernel(lax.axis_size("ctx"), extent, *refs),
        out_shape=(jax.ShapeDtypeStruct((tok, groups * per_group, size), half), grads, grads),
        in_specs=[hbm, vmem],
        out_specs=(hbm, vmem, vmem),
        scratch_shapes=[
            pltpu.VMEM((2, extent, members, tok, size), half),
            pltpu.VMEM((2, 2, 4) + end, half),
            pltpu.VMEM((2, 2, 4) + whole, half),
            pltpu.VMEM((2, 2, 4) + end, half),
            pltpu.VMEM((2, 2, 4) + whole, half),
            pltpu.VMEM((2,) + end, half),
            pltpu.VMEM((2,) + end, half),
            pltpu.VMEM((2,) + whole, half),
            pltpu.VMEM((2,) + whole, half),
            pltpu.VMEM((2, tok, groups, size), jnp.float32),
            pltpu.SemaphoreType.DMA((2, groups - 1)),
            pltpu.SemaphoreType.DMA((2, groups - 1)),
            pltpu.SemaphoreType.DMA((2,)),
            pltpu.SemaphoreType.DMA((2, 2, 2, 4)),
            pltpu.SemaphoreType.DMA((2, 2, 2, 4)),
            pltpu.SemaphoreType.DMA((2, members)),
            pltpu.SemaphoreType.DMA((2, members)),
            pltpu.SemaphoreType.DMA((2,)),
            pltpu.SemaphoreType.DMA((2,)),
        ],
        compiler_params=pltpu.CompilerParams(
            collective_id=1, has_side_effects=True, vmem_limit_bytes=28 * 2**20
        ),
    )(dq_rows, dkv)


def per_device(queries, keys, values, outputs, out_grads, log_norms, block_doc):
    tok, heads_all, size = queries.shape
    groups = keys.shape[1]
    per_group = heads_all // groups
    members = lax.axis_size("head") // groups
    extent = groups
    there = [
        pltpu.with_memory_space_constraint(array, pltpu.HBM)
        for array in (queries, out_grads, outputs, keys, values, log_norms)
    ]
    q_rows, g_rows, kv, stats = gather(extent, *there, members)
    rows = (groups, tok * per_group, size)
    dq_rows, dkv = attention(
        pltpu.with_memory_space_constraint(block_doc, pltpu.HBM),
        q_rows.reshape(rows),
        g_rows.reshape(rows),
        stats,
        kv.reshape(2, -1, size),
        members,
    )
    return reduce(extent, dq_rows.reshape(q_rows.shape), dkv.reshape(kv.shape))


def solution(mesh):
    tokens = P(("ctx", "head"), None, None)
    return jax.shard_map(
        per_device,
        mesh=mesh,
        in_specs=(tokens, tokens, tokens, tokens, tokens, P(("ctx", "head"), None), P()),
        out_specs=(tokens, tokens, tokens),
        check_vma=False,
    )
```
